32 devices in a mesh: gx: 4 (over z), gy: 2 (over x), gz: 4 (over y, core).
Axes of the slice: x: 2, y: 2, z: 4, core: 2. Of those that a mesh axis runs over, the one named last changes fastest.
Arguments:
- final_adjoint: float32 [9, 56, 4096], P(None, None, ('gx', 'gy', 'gz')), may hold values from -6 to 6
- star_mats: float32 [3, 9, 9, 4096], P(None, None, None, ('gx', 'gy', 'gz')), may hold values from -6 to 6
- deriv_stiff: float32 [3, 56, 56], replicated, may hold values from -6 to 6
- volume_stiffness: float32 [3, 56, 56], replicated, may hold values from -0.21875 to 0.21875
- face_projection: float32 [4, 21, 56], replicated, may hold values from -0.75 to 0.75
- flux_local: float32 [4, 9, 9, 4096], P(None, None, None, ('gx', 'gy', 'gz')), may hold values from -0.875 to 0.875
- flux_across: float32 [4, 9, 9, 4096], P(None, None, None, ('gx', 'gy', 'gz')), may hold values from -0.875 to 0.875
- cluster: int32 [4096], P(('gx', 'gy', 'gz')), may hold values from 0 to 1, as said below
- partner: int32 [4, 4096], P(None, ('gx', 'gy', 'gz')), may hold values from 0 to 703, as said below
- send_slots: int32 [6, 1024], P(None, ('gx', 'gy', 'gz')), may hold values from 0 to 511, as said below
Outputs:
- initial_adjoint: float32 [9, 56, 4096], P(None, None, ('gx', 'gy', 'gz'))
The draws below stay inside these ranges and needn't reach their ends.
Inputs may be any that keep to these rules, and one draw needn't show every extreme that they name: At most 64 of a partition's elements have cluster 0, some partition has exactly 64, and every partition has at least three sixteenths of 128. `send_slots`: row d of a partition lists 32 distinct face slots c * 128 + e lying on its boundary toward direction d; no slot is in two rows. At most 16 slots of a row belong to cluster-0 elements, and some row of some partition has exactly 16. partner[c, e] = 512 + d * 32 + j exactly when send_slots[d, j] of the partition is c * 128 + e; every other slot's partner is another slot of the same partition below 512 whose partner is it.
All inputs are finite; a program needn't handle non-finite values.
Results may differ from the reference program's by a relative error of at most 0.0003.
Values sent between devices are 32-bit elements; how exact they have to be, the bound alone decides.
No kernel may reach another device: no remote copies, remote signals or barrier semaphores. Data moves between devices by JAX's collectives and lax.ppermute only.
A program may use at most 64 MiB of HBM per device.

```python
import math
import jax
import jax.numpy as jnp
from jax import lax

FIELDS = 9
MODES = 56
FACE_MODES = 21
TERMS = 6
FINE_STEPS = 4
E_DEV = 128
ELEMS = 4096
N_GX = 4
N_GY = 2
N_GZ = 4


def shuffled_slots(key):
    return jax.random.permutation(key, E_DEV // 4)


def partition_topology(key, starred, star_side):
    members = E_DEV
    width = members // 4
    most = width // 2
    streams = jax.random.split(key, 6)
    fast_count = jax.random.randint(streams[0], (), members * 3 // 16, members // 2 + 1)
    fast_count = jnp.where(starred, members // 2, fast_count)
    ranking = jnp.zeros((members,), jnp.int32).at[jax.random.permutation(streams[1], members)].set(jnp.arange(members, dtype=jnp.int32))
    kinds = (ranking >= fast_count).astype(jnp.int32)
    mixing = jax.random.permutation(streams[2], 4 * members)
    sorted_faces = mixing[jnp.argsort(kinds[mixing % members], stable=True)]
    per_side = jax.random.randint(streams[3], (6,), most // 2, most + 1)
    per_side = jnp.where(starred & (jnp.arange(6) == star_side), most, per_side)
    fast_start = jnp.cumsum(per_side) - per_side
    slow_start = jnp.cumsum(width - per_side) - (width - per_side) + 4 * fast_count
    column = jnp.arange(width, dtype=jnp.int32)[None, :]
    fast_pick = jnp.clip(fast_start[:, None] + column, 0, 4 * members - 1)
    slow_pick = jnp.clip(slow_start[:, None] + column - per_side[:, None], 0, 4 * members - 1)
    chosen = jnp.where(column < per_side[:, None], sorted_faces[fast_pick], sorted_faces[slow_pick])
    shuffles = jax.vmap(shuffled_slots)(jax.random.split(streams[4], 6))
    listing = jnp.take_along_axis(chosen, shuffles, axis=1).astype(jnp.int32)
    flat_list = listing.reshape(-1)
    remote = jnp.zeros((4 * members,), jnp.int32).at[flat_list].set(1)
    scramble = jax.random.permutation(streams[5], 4 * members)
    lined = scramble[jnp.argsort(remote[scramble], stable=True)]
    paired = 4 * members - 6 * width
    first_side = lined[0:paired:2]
    second_side = lined[1:paired:2]
    links = jnp.zeros((4 * members,), jnp.int32).at[first_side].set(second_side).at[second_side].set(first_side)
    links = links.at[flat_list].set(4 * members + jnp.arange(6 * width, dtype=jnp.int32))
    return (kinds, links.reshape(4, members), listing)


def mesh_topology(key):
    base = jax.random.fold_in(key, 7)
    groups = ELEMS // E_DEV
    starred_group = jax.random.randint(jax.random.fold_in(base, 1), (), 0, groups)
    star_side = jax.random.randint(jax.random.fold_in(base, 2), (), 0, 6)
    group_keys = jax.random.split(jax.random.fold_in(base, 3), groups)
    marks = jnp.arange(groups) == starred_group
    kinds, links, listing = jax.vmap(partition_topology, in_axes=(0, 0, None))(group_keys, marks, star_side)
    kinds = kinds.reshape(-1)
    links = jnp.transpose(links, (1, 0, 2)).reshape(4, -1)
    listing = jnp.transpose(listing, (1, 0, 2)).reshape(6, -1)
    return (kinds, links, listing)


def draw_cluster(key, part):
    return mesh_topology(key)[0]


def draw_partner(key, part):
    return mesh_topology(key)[1]


def draw_send_slots(key, part):
    return mesh_topology(key)[2]


def draw_star_mats(key, part):
    kinds = mesh_topology(key)[0]
    speed = jnp.where(kinds == 0, 1.0, 0.25).astype(jnp.float32)
    inner = jax.random.fold_in(key, 11)
    raw = jax.random.truncated_normal(inner, -4.0, 4.0, (3, FIELDS, FIELDS, ELEMS), jnp.float32)
    return (raw + jnp.transpose(raw, (0, 2, 1, 3))) * (0.7 * speed)


def draw_deriv_stiff(key, part):
    inner = jax.random.fold_in(key, 13)
    raw = jax.random.truncated_normal(inner, -4.0, 4.0, (3, MODES, MODES), jnp.float32)
    return (raw - jnp.transpose(raw, (0, 2, 1))) * (0.7 / math.sqrt(MODES))


def block_scale(stream_key, dims, cuts, smallest, high):
    def one(dim, shards_of):
        draws = jax.random.uniform(jax.random.fold_in(jax.random.fold_in(stream_key, 6), dim), (shards_of,), jnp.float32, smallest / len(cuts), high / len(cuts))
        return jnp.repeat(jnp.exp(draws), dims[dim] // shards_of).reshape((-1,) + (1,) * (len(dims) - dim - 1))

    loudness = one(*cuts[0])
    for cut in cuts[1:]:
        loudness = loudness * one(*cut)
    return loudness


def normal_values(stream_key, extent, deviation, bound, cuts=(), kind=jnp.bfloat16):
    loudness = block_scale(stream_key, extent, cuts, -0.22, 0.18) if cuts else 1.0
    entries = jax.random.normal(stream_key, extent, jnp.float32) * deviation * loudness
    return jnp.minimum(jnp.maximum(entries, -bound), bound).astype(kind)


def setup_inputs(seed: int = 0) -> dict:
    splits = jax.random.split(jax.random.key(seed), 11)
    final_adjoint = normal_values(splits[0], (FIELDS, MODES, ELEMS), 1.0, 6.0, ((2, 32),), jnp.float32)
    star_mats = draw_star_mats(jax.random.fold_in(splits[10], 71), 0)
    deriv_stiff = draw_deriv_stiff(jax.random.fold_in(splits[10], 71), 0)
    volume_stiffness = normal_values(splits[3], (3, MODES, MODES), 0.035, 0.21875, (), jnp.float32)
    face_projection = normal_values(splits[4], (4, FACE_MODES, MODES), MODES ** -0.5, 0.75, (), jnp.float32)
    flux_local = normal_values(splits[5], (4, FIELDS, FIELDS, ELEMS), 0.15, 0.875, ((3, 32),), jnp.float32)
    flux_across = normal_values(splits[6], (4, FIELDS, FIELDS, ELEMS), 0.15, 0.875, ((3, 32),), jnp.float32)
    cluster = draw_cluster(jax.random.fold_in(splits[10], 71), 0)
    partner = draw_partner(jax.random.fold_in(splits[10], 71), 0)
    send_slots = draw_send_slots(jax.random.fold_in(splits[10], 71), 0)
    return {"final_adjoint": final_adjoint, "star_mats": star_mats, "deriv_stiff": deriv_stiff, "volume_stiffness": volume_stiffness, "face_projection": face_projection, "flux_local": flux_local, "flux_across": flux_across, "cluster": cluster, "partner": partner, "send_slots": send_slots}


HIGH_ORDER = lax.Precision.HIGHEST


def coefficients(lower, upper):
    return [(upper ** (k + 1) - lower ** (k + 1)) / math.factorial(k + 1) for k in range(TERMS)]


def derive_terms(value_rows, stiff, matrix_list):
    turned = jnp.einsum("dmn,fme->dfne", stiff, value_rows, precision=HIGH_ORDER)
    return jnp.einsum("dgfe,dfne->gne", matrix_list, turned, precision=HIGH_ORDER)


def face_terms(adjoint, face_projection, flux_local, flux_across):
    traces = jnp.einsum("cbm,fme->fbce", face_projection, adjoint, precision=HIGH_ORDER)
    own_element = jnp.einsum("cgfe,fbce->gbce", flux_local, traces, precision=HIGH_ORDER)
    sent = jnp.einsum("cgfe,fbce->gbce", flux_across, traces, precision=HIGH_ORDER)
    return own_element, sent


def blocks(array, groups):
    leading = array.shape[:-1]
    split = array.reshape(leading + (groups, -1))
    return jnp.moveaxis(split, -2, 0)


def unblocks(array):
    joined = jnp.moveaxis(array, 0, -2)
    return joined.reshape(joined.shape[:-2] + (-1,))


def from_lower(value_rows, axis):
    widths = [(0, 0)] * value_rows.ndim
    widths[axis] = (1, 0)
    return lax.slice_in_dim(jnp.pad(value_rows, widths), 0, value_rows.shape[axis], axis=axis)


def from_upper(value_rows, axis):
    widths = [(0, 0)] * value_rows.ndim
    widths[axis] = (0, 1)
    return lax.slice_in_dim(jnp.pad(value_rows, widths), 1, value_rows.shape[axis] + 1, axis=axis)


def neighbours(boxes):
    grid = boxes.reshape((N_GX, N_GY, N_GZ) + boxes.shape[1:])
    pieces = [from_lower(grid[..., 1, :], 0), from_upper(grid[..., 0, :], 0),
              from_lower(grid[..., 3, :], 1), from_upper(grid[..., 2, :], 1),
              from_lower(grid[..., 5, :], 2), from_upper(grid[..., 4, :], 2)]
    stacked = jnp.stack(pieces, axis=-2)
    return stacked.reshape((boxes.shape[0], boxes.shape[1], -1))


def horner_rows(source_field, rows, stiff, matrix_list):
    total = rows[TERMS - 1] * source_field
    for k in range(TERMS - 2, -1, -1):
        total = rows[k] * source_field + derive_terms(total, stiff, matrix_list)
    return total


def reference(final_adjoint, star_mats, deriv_stiff, volume_stiffness, face_projection, flux_local, flux_across, cluster, partner, send_slots):
    groups = N_GX * N_GY * N_GZ
    fine = 1.0 / FINE_STEPS
    adjoint = blocks(final_adjoint, groups)
    mats_all = blocks(star_mats, groups)
    local_all = blocks(flux_local, groups)
    across_all = blocks(flux_across, groups)
    kinds_all = blocks(cluster, groups)
    links_all = blocks(partner, groups)
    lists_all = blocks(send_slots, groups)
    store = jnp.zeros_like(adjoint)
    fast_rows = coefficients(0.0, fine)
    for step in range(FINE_STEPS - 1, -1, -1):
        slow_rows = coefficients(step * fine, (step + 1) * fine)

        def outgoing(entry):
            value_rows, local_mats, across_mats, listing = entry
            own_element, sent = face_terms(value_rows, face_projection, local_mats, across_mats)
            sent_flat = sent.reshape(sent.shape[0] * sent.shape[1], -1)
            return jnp.take(sent_flat, listing, axis=1)

        boxes = lax.map(outgoing, (adjoint, local_all, across_all, lists_all))
        received = neighbours(boxes)

        def advance(entry):
            value_rows, matrix_list, local_mats, across_mats, kinds, links, arrived, kept = entry
            own_element, sent = face_terms(value_rows, face_projection, local_mats, across_mats)
            sent_flat = sent.reshape(sent.shape[0] * sent.shape[1], -1)
            extended = jnp.concatenate([sent_flat, arrived], axis=1)
            incoming_flux = jnp.take(extended, links.reshape(-1).astype(jnp.int32), axis=1).reshape(own_element.shape)
            source_field = derive_terms(value_rows, volume_stiffness, matrix_list) + jnp.einsum("mpu,apmx->aux", face_projection, own_element + incoming_flux, precision=HIGH_ORDER)
            rows = [jnp.where(kinds == 0, fast_rows[k], slow_rows[k]) for k in range(TERMS)]
            change = horner_rows(source_field, rows, deriv_stiff, matrix_list)
            fast_share = (kinds == 0).astype(jnp.float32)
            return value_rows + change * fast_share, kept + change * (1.0 - fast_share)

        adjoint, store = lax.map(advance, (adjoint, mats_all, local_all, across_all, kinds_all, links_all, received, store))
    return unblocks(adjoint + store)
```

```python
import math

import jax
import jax.numpy as jnp
from jax import lax
from jax.sharding import PartitionSpec as P

TERMS = 6
FINE_STEPS = 4


HIGH_ORDER = lax.Precision.HIGHEST


AXES = ("gx", "gy", "gz")


def matchings():
    plan = []
    for axis in AXES:
        size = lax.axis_size(axis)
        for first in (0, 1):
            links = [(i, i + 1) for i in range(first, size - 1, 2)]
            if not links:
                continue
            if first == 1 and size % 2 == 0:
                links.append((size - 1, 0))
            plan.append((axis, [q for i, j in links for q in ((i, j), (j, i))], first))
    return plan


def routes(plan, send_slots, partner, members):
    width = send_slots.shape[1]
    lists, block = [], [None] * 6
    for number, (axis, _, first) in enumerate(plan):
        a, place, size = AXES.index(axis), lax.axis_index(axis), lax.axis_size(axis)
        upward = place % 2 == first
        lists.append(jnp.where(upward, send_slots[2 * a + 1], send_slots[2 * a]))
        for side, chosen in ((0, ~upward), (1, upward)):
            d = 2 * a + side
            real = chosen & ((place > 0) if side == 0 else (place < size - 1))
            before = block[d] if block[d] is not None else len(plan)
            block[d] = jnp.where(real, number, before)
    block = jnp.stack([jnp.int32(len(plan)) if b is None else b.astype(jnp.int32) for b in block])
    far = partner - 4 * members
    d, j = far // width, far % width
    moved = sum(jnp.where(d == i, block[i], 0) for i in range(6)) * width + j + 4 * members
    return jnp.stack(lists), jnp.where(far < 0, partner, moved)


def trade_every(plan, boxes):
    got = [lax.ppermute(boxes[:, i], axis, pairs) for i, (axis, pairs, _) in enumerate(plan)]
    return jnp.stack(got + [jnp.zeros_like(boxes[:, 0])], axis=1)


def coefficients(lower, upper):
    return [(upper ** (k + 1) - lower ** (k + 1)) / math.factorial(k + 1) for k in range(TERMS)]


def derive_terms(value_rows, stiff, matrix_list):
    turned = jnp.einsum("dmn,fme->dfne", stiff, value_rows, precision=HIGH_ORDER)
    return jnp.sum(matrix_list[:, :, :, None, :] * turned[:, None, :, :, :], axis=(0, 2))


def face_terms(adjoint, face_projection, flux_local, flux_across):
    traces = jnp.einsum("cbm,fme->cfbe", face_projection, adjoint, precision=HIGH_ORDER)
    own_element = jnp.sum(flux_local[:, :, :, None, :] * traces[:, None, :, :, :], axis=2)
    sent = jnp.sum(flux_across[:, :, :, None, :] * traces[:, None, :, :, :], axis=2)
    return (jnp.transpose(own_element, (1, 2, 0, 3)), jnp.transpose(sent, (1, 2, 0, 3)))


def horner_rows(source_field, rows, stiff, matrix_list):
    total = rows[TERMS - 1] * source_field
    for k in range(TERMS - 2, -1, -1):
        total = rows[k] * source_field + derive_terms(total, stiff, matrix_list)
    return total


def body(
    final_adjoint,
    star_mats,
    deriv_stiff,
    volume_stiffness,
    face_projection,
    flux_local,
    flux_across,
    cluster,
    partner,
    send_slots,
):
    fields, modes, members = final_adjoint.shape
    fine = 1.0 / FINE_STEPS
    is_fast = cluster == 0
    fast_share = is_fast.astype(jnp.float32)
    slow_share = 1.0 - fast_share
    fast_rows = coefficients(0.0, fine)
    plan = matchings()
    send_list, table = routes(plan, send_slots, partner, members)
    flat_partner = table.reshape(-1)
    adjoint = final_adjoint
    store = jnp.zeros_like(final_adjoint)
    for step in range(FINE_STEPS - 1, -1, -1):
        slow_rows = coefficients(step * fine, (step + 1) * fine)
        own_element, sent = face_terms(adjoint, face_projection, flux_local, flux_across)
        sent_flat = sent.reshape(fields * sent.shape[1], 4 * members)
        received = trade_every(plan, jnp.take(sent_flat, send_list, axis=1))
        extended = jnp.concatenate([sent_flat, received.reshape(sent_flat.shape[0], -1)], axis=1)
        incoming_flux = jnp.take(extended, flat_partner, axis=1).reshape(own_element.shape)
        source_field = derive_terms(adjoint, volume_stiffness, star_mats) + jnp.einsum(
            "mpu,apmx->aux", face_projection, own_element + incoming_flux, precision=HIGH_ORDER
        )
        rows = [jnp.where(is_fast, fast_rows[k], slow_rows[k]) for k in range(TERMS)]
        change = horner_rows(source_field, rows, deriv_stiff, star_mats)
        adjoint = adjoint + change * fast_share
        store = store + change * slow_share
    return adjoint + store


def solution(mesh):
    in_specs = (
        P(None, None, ("gx", "gy", "gz")),
        P(None, None, None, ("gx", "gy", "gz")),
        P(),
        P(),
        P(),
        P(None, None, None, ("gx", "gy", "gz")),
        P(None, None, None, ("gx", "gy", "gz")),
        P(("gx", "gy", "gz")),
        P(None, ("gx", "gy", "gz")),
        P(None, ("gx", "gy", "gz")),
    )
    out_specs = P(None, None, ("gx", "gy", "gz"))
    return jax.shard_map(body, mesh=mesh, in_specs=in_specs, out_specs=out_specs, check_vma=False)
```

```python
import functools
import math

import jax
import jax.numpy as jnp
from jax import lax
from jax.experimental import pallas as pl
from jax.experimental.pallas import tpu as pltpu
from jax.sharding import PartitionSpec as P

TERMS = 6
FINE_STEPS = 4
BF = jnp.bfloat16
F32 = jnp.float32


def up(n, unit):
    return -(-n // unit) * unit


AXES = ("gx", "gy", "gz")


def matchings():
    plan = []
    for axis in AXES:
        size = lax.axis_size(axis)
        for first in (0, 1):
            links = [(i, i + 1) for i in range(first, size - 1, 2)]
            if not links:
                continue
            if first == 1 and size % 2 == 0:
                links.append((size - 1, 0))
            plan.append((axis, [q for i, j in links for q in ((i, j), (j, i))], first))
    return plan


def routes(plan, send_slots, partner, members):
    width = send_slots.shape[1]
    lists, block = [], [None] * 6
    for number, (axis, _, first) in enumerate(plan):
        a, place, size = AXES.index(axis), lax.axis_index(axis), lax.axis_size(axis)
        upward = place % 2 == first
        lists.append(jnp.where(upward, send_slots[2 * a + 1], send_slots[2 * a]))
        for side, chosen in ((0, ~upward), (1, upward)):
            d = 2 * a + side
            real = chosen & ((place > 0) if side == 0 else (place < size - 1))
            before = block[d] if block[d] is not None else len(plan)
            block[d] = jnp.where(real, number, before)
    block = jnp.stack([jnp.int32(len(plan)) if b is None else b.astype(jnp.int32) for b in block])
    far = partner - 4 * members
    d, j = far // width, far % width
    moved = sum(jnp.where(d == i, block[i], 0) for i in range(6)) * width + j + 4 * members
    return jnp.stack(lists), jnp.where(far < 0, partner, jnp.where(moved < 4 * members + len(plan) * width, moved, -1))


def coefficients(lower, upper):
    return [(upper ** (k + 1) - lower ** (k + 1)) / math.factorial(k + 1) for k in range(TERMS)]


def halves(x):
    hi = x.astype(BF)
    return hi, (x - hi.astype(F32)).astype(BF)


def triple(matrix):
    hi = lax.reduce_precision(matrix, 8, 7)
    lo = (matrix - hi).astype(BF)
    hi = hi.astype(BF)
    return jnp.concatenate([hi, hi, lo], axis=1)


def dot(a, b):
    return jnp.dot(a, b, preferred_element_type=F32)


class Sizes:
    def __init__(self, fields, modes, faces, bases, members, width, messages):
        self.F, self.M, self.C, self.B, self.E = fields, modes, faces, bases, members
        self.W, self.K = width, messages
        self.MP = up(modes, 16)
        self.BP = up(bases, 8)
        self.BQ = up(bases, 16)
        self.R = fields * self.BP
        self.RP = up(self.R, 16)
        self.Q = members // width
        self.QR = up(up(self.R, 8 * self.Q) // self.Q, 8)
        self.KW = up(messages * width, 128)
        self.S = faces * members


def put_field(z, y3, f, x):
    hi, lo = halves(x)
    lanes = slice(f * z.E, (f + 1) * z.E)
    y3[0:z.M, lanes] = hi
    y3[z.MP:z.MP + z.M, lanes] = lo
    y3[2 * z.MP:2 * z.MP + z.M, lanes] = hi


def star_sum(z, start, group, turned, star):
    total = list(start)
    for f in range(z.F):
        for d in range(3):
            t = turned[d * z.M:(d + 1) * z.M, f * z.E:(f + 1) * z.E]
            for i, g in enumerate(group):
                total[i] = total[i] + star[g, f, d:d + 1, :] * t
    return total


def groups_of(n, size):
    return [list(range(i, min(n, i + size))) for i in range(0, n, size)]


def send_part(z, y3, p3, across, ohs, sx, messages, traces, sent, picked):
    traces[...] = dot(p3[...], y3[...])
    for c in range(z.C):
        rows = slice(c * z.BP, (c + 1) * z.BP)
        t = [traces[rows, f * z.E:(f + 1) * z.E] for f in range(z.F)]
        for g in range(z.F):
            total = across[g, 0, c:c + 1, :] * t[0]
            for f in range(1, z.F):
                total = total + across[g, f, c:c + 1, :] * t[f]
            sent[g * z.BP:(g + 1) * z.BP, c * z.E:(c + 1) * z.E] = total
    hi, lo = halves(sent[...])
    sx[0:z.R, :] = hi
    sx[z.RP:z.RP + z.R, :] = lo
    both = dot(sx[...], ohs[...])
    picked[...] = both[0:z.R, :] + both[z.RP:z.RP + z.R, :]
    for m, message in enumerate(messages):
        for q in range(z.Q):
            rows = min(z.R, (q + 1) * z.QR) - q * z.QR
            lanes = slice(q * z.W, (q + 1) * z.W)
            message[0:rows, lanes] = picked[q * z.QR:q * z.QR + rows, m * z.W:(m + 1) * z.W]
            if rows < z.QR:
                message[rows:z.QR, lanes] = jnp.zeros((z.QR - rows, z.W), F32)


def first_kernel(z, y, p3, across, ohs, *rest):
    sx, messages = rest[0], rest[1:1 + z.K]
    y3, traces, sent, picked = rest[1 + z.K:]
    y3[...] = jnp.zeros_like(y3)
    for f in range(z.F):
        put_field(z, y3, f, y[f * z.M:(f + 1) * z.M, :])
    send_part(z, y3, p3, across, ohs, sx, messages, traces, sent, picked)


def local_kernel(z, y, svp, pt, star, local, sx, ohl, src, y3, turned, u, gathered):
    y3[...] = jnp.zeros_like(y3)
    u[...] = jnp.zeros_like(u)
    for f in range(z.F):
        put_field(z, y3, f, y[f * z.M:(f + 1) * z.M, :])
    turned[...] = dot(svp[...], y3[...])
    gathered[...] = dot(sx[...], ohl[...])
    top = 3 * z.M
    for c in range(z.C):
        rows = slice(top + c * z.BP, top + (c + 1) * z.BP)
        t = [turned[rows, f * z.E:(f + 1) * z.E] for f in range(z.F)]
        for g in range(z.F):
            slots = slice(c * z.E, (c + 1) * z.E)
            total = gathered[g * z.BP:(g + 1) * z.BP, slots] + gathered[z.RP + g * z.BP:z.RP + (g + 1) * z.BP, slots]
            for f in range(z.F):
                total = total + local[g, f, c:c + 1, :] * t[f]
            hi, lo = halves(total)
            lanes = slice(g * z.E, (g + 1) * z.E)
            for part, value in enumerate((hi, lo, hi)):
                at = (part * z.C + c) * z.BQ
                u[at:at + z.BP, lanes] = value
    lifted = dot(pt[...], u[...])
    for group in groups_of(z.F, 3):
        start = [lifted[:, g * z.E:(g + 1) * z.E] for g in group]
        for g, total in zip(group, star_sum(z, start, group, turned, star)):
            src[g * z.M:(g + 1) * z.M, :] = total


def step_kernel(z, last, *refs):
    arrived, refs = refs[:z.K], refs[z.K:]
    total_in, y, src_local, coef, s3, pt, star, ohr = refs[:8]
    refs = refs[8:]
    if last:
        total_out = refs[0]
        refs = refs[1:]
    else:
        p3, across, ohs, total_out, y_out, sx = refs[:6]
        messages = refs[6:6 + z.K]
        refs = refs[6 + z.K:]
    y3, turned, u, gathered, landed, stacked, src, change = refs[:8]
    y3[...] = jnp.zeros_like(y3)
    u[...] = jnp.zeros_like(u)
    landed[...] = jnp.zeros_like(landed)
    for m in range(z.K):
        for q in range(z.Q):
            rows = min(z.R, (q + 1) * z.QR) - q * z.QR
            landed[q * z.QR:q * z.QR + rows, m * z.W:(m + 1) * z.W] = arrived[m][0:rows, q * z.W:(q + 1) * z.W]
    hi, lo = halves(landed[...])
    stacked[0:z.R, :] = hi
    stacked[z.RP:z.RP + z.R, :] = lo
    gathered[...] = dot(stacked[...], ohr[...])
    for c in range(z.C):
        slots = slice(c * z.E, (c + 1) * z.E)
        for g in range(z.F):
            lanes = slice(g * z.E, (g + 1) * z.E)
            hi = gathered[g * z.BP:(g + 1) * z.BP, slots].astype(BF)
            lo = gathered[z.RP + g * z.BP:z.RP + (g + 1) * z.BP, slots].astype(BF)
            for part, value in enumerate((hi, lo, hi)):
                at = (part * z.C + c) * z.BQ
                u[at:at + z.BP, lanes] = value
    lifted = dot(pt[...], u[...])
    for g in range(z.F):
        value = src_local[g * z.M:(g + 1) * z.M, :] + lifted[:, g * z.E:(g + 1) * z.E]
        src[g * z.M:(g + 1) * z.M, :] = value
        put_field(z, y3, g, coef[TERMS - 1:TERMS, :] * value)

    def term(i, carry):
        row = coef[pl.ds(TERMS - 2 - i, 1), :]
        turned[...] = dot(s3[...], y3[...])
        for group in groups_of(z.F, 3):
            start = [row * src[g * z.M:(g + 1) * z.M, :] for g in group]
            for g, total in zip(group, star_sum(z, start, group, turned, star)):
                put_field(z, y3, g, total)
                change[g * z.M:(g + 1) * z.M, :] = total
        return carry

    lax.fori_loop(0, TERMS - 1, term, 0)
    total_out[...] = total_in[...] + change[...]
    if last:
        return
    traces, sent, picked = refs[8:]
    for f in range(z.F):
        rows = slice(f * z.M, (f + 1) * z.M)
        value = y[rows, :] + coef[TERMS:TERMS + 1, :] * change[rows, :]
        y_out[rows, :] = value
        put_field(z, y3, f, value)
    send_part(z, y3, p3, across, ohs, sx, messages, traces, sent, picked)


def call(z, kernel, outs, scratch, flops, *args):
    spec = pl.BlockSpec(memory_space=pltpu.VMEM)
    return pl.pallas_call(
        kernel,
        out_shape=[jax.ShapeDtypeStruct(*o) for o in outs],
        in_specs=[spec] * len(args),
        out_specs=[spec] * len(outs),
        scratch_shapes=[pltpu.VMEM(*o) for o in scratch],
        compiler_params=pltpu.CompilerParams(vmem_limit_bytes=24 << 20),
        cost_estimate=pl.CostEstimate(flops=flops, bytes_accessed=2 << 20, transcendentals=0),
    )(*args)


def body(
    final_adjoint,
    star_mats,
    deriv_stiff,
    volume_stiffness,
    face_projection,
    flux_local,
    flux_across,
    cluster,
    partner,
    send_slots,
):
    fields, modes, members = final_adjoint.shape
    faces, bases, _ = face_projection.shape
    plan = matchings()
    send_list, table = routes(plan, send_slots, partner, members)
    width = send_slots.shape[1]
    z = Sizes(fields, modes, faces, bases, members, width, len(plan))

    def stiff(matrices):
        rows = jnp.transpose(matrices, (0, 2, 1)).reshape(3 * modes, modes)
        return triple(jnp.pad(rows, ((0, 0), (0, z.MP - modes))))

    s3 = stiff(deriv_stiff)
    projection = jnp.pad(face_projection, ((0, 0), (0, z.BP - bases), (0, z.MP - modes)))
    p3 = triple(projection.reshape(faces * z.BP, z.MP))
    svp = jnp.concatenate([stiff(volume_stiffness), p3], axis=0)
    lift = jnp.pad(face_projection, ((0, 0), (0, z.BQ - bases), (0, 0)))
    pt = triple(jnp.transpose(lift.reshape(faces * z.BQ, modes)))
    star = jnp.transpose(star_mats, (1, 2, 0, 3))
    local = jnp.transpose(flux_local, (1, 2, 0, 3))
    across = jnp.transpose(flux_across, (1, 2, 0, 3))
    picks = jnp.pad(send_list.reshape(-1), (0, z.KW - z.K * width), constant_values=-1)
    slots = table.reshape(-1)
    ohs = (lax.broadcasted_iota(jnp.int32, (z.S, z.KW), 0) == picks[None, :]).astype(BF)
    ohl = (lax.broadcasted_iota(jnp.int32, (z.S, z.S), 0) == slots[None, :]).astype(BF)
    ohr = (lax.broadcasted_iota(jnp.int32, (z.KW, z.S), 0) + z.S == slots[None, :]).astype(BF)
    fast = (cluster == 0)[None, :]
    fine = 1.0 / FINE_STEPS
    coefs = []
    for step in range(FINE_STEPS):
        pairs = zip(coefficients(0.0, fine), coefficients(step * fine, (step + 1) * fine))
        rows = [jnp.where(fast, F32(a), F32(b)) for a, b in pairs]
        coefs.append(jnp.concatenate(rows + [fast.astype(F32), jnp.zeros((1, members), F32)], axis=0))

    field = ((fields * modes, members), F32)
    sx_out = ((2 * z.RP, z.S), BF)
    message_outs = [((z.QR, members), F32)] * z.K
    y3 = ((3 * z.MP, fields * members), BF)
    u = ((3 * faces * z.BQ, fields * members), BF)
    gathered = ((2 * z.RP, z.S), F32)
    send_scratch = [((faces * z.BP, fields * members), F32), ((z.R, z.S), F32), ((z.R, z.KW), F32)]

    def trade(messages):
        return [lax.ppermute(m, axis, pairs) for m, (axis, pairs, _) in zip(messages, plan)]

    y = total = final_adjoint.reshape(fields * modes, members)
    sx, *messages = call(z, functools.partial(first_kernel, z), [sx_out] + message_outs, [y3] + send_scratch, 1 << 28, y, p3, across, ohs)
    for step in range(FINE_STEPS - 1, -1, -1):
        arrived = trade(messages)
        (src,) = call(
            z, functools.partial(local_kernel, z), [field],
            [y3, ((3 * modes + faces * z.BP, fields * members), F32), u, gathered], 1 << 30,
            y, svp, pt, star, local, sx, ohl,
        )
        scratch = [y3, ((3 * modes, fields * members), F32), u, gathered, ((z.R, z.KW), F32), ((2 * z.RP, z.KW), BF), field, field]
        args = arrived + [total, y, src, coefs[step], s3, pt, star, ohr]
        if step == 0:
            (total,) = call(z, functools.partial(step_kernel, z, True), [field], scratch, 1 << 30, *args)
        else:
            total, y, sx, *messages = call(
                z, functools.partial(step_kernel, z, False), [field, field, sx_out] + message_outs,
                scratch + send_scratch, 1 << 30, *args, p3, across, ohs,
            )
    return total.reshape(fields, modes, members)


def solution(mesh):
    in_specs = (
        P(None, None, ("gx", "gy", "gz")),
        P(None, None, None, ("gx", "gy", "gz")),
        P(),
        P(),
        P(),
        P(None, None, None, ("gx", "gy", "gz")),
        P(None, None, None, ("gx", "gy", "gz")),
        P(("gx", "gy", "gz")),
        P(None, ("gx", "gy", "gz")),
        P(None, ("gx", "gy", "gz")),
    )
    out_specs = P(None, None, ("gx", "gy", "gz"))
    return jax.shard_map(body, mesh=mesh, in_specs=in_specs, out_specs=out_specs, check_vma=False)
```

```python
import functools
import math

import jax
import jax.numpy as jnp
from jax import lax
from jax.experimental import pallas as pl
from jax.experimental.pallas import tpu as pltpu
from jax.sharding import PartitionSpec as P

TERMS = 6
FINE_STEPS = 4
BF = jnp.bfloat16
F32 = jnp.float32


def up(n, unit):
    return -(-n // unit) * unit


AXES = ("gx", "gy", "gz")


def matchings():
    plan = []
    for axis in AXES:
        size = lax.axis_size(axis)
        for first in (0, 1):
            links = [(i, i + 1) for i in range(first, size - 1, 2)]
            if not links:
                continue
            if first == 1 and size % 2 == 0:
                links.append((size - 1, 0))
            plan.append((axis, [q for i, j in links for q in ((i, j), (j, i))], first))
    return plan


def bearings(plan):
    upward, block = [], [jnp.int32(-1)] * 6
    for number, (axis, _, first) in enumerate(plan):
        a, place, size = AXES.index(axis), lax.axis_index(axis), lax.axis_size(axis)
        rises = lax.rem(place, 2) == first
        upward.append((a, rises))
        for side in (0, 1):
            inside = (place > 0) if side == 0 else (place < size - 1)
            used = jnp.logical_and(rises if side == 1 else jnp.logical_not(rises), inside)
            block[2 * a + side] = jnp.where(used, number, block[2 * a + side])
    return upward, block


def coefficients(lower, upper):
    return [(upper ** (k + 1) - lower ** (k + 1)) / math.factorial(k + 1) for k in range(TERMS)]


def halves(x):
    hi = x.astype(BF)
    return hi, (x - hi.astype(F32)).astype(BF)


def dot(a, b):
    return jnp.dot(a, b, preferred_element_type=F32)


class Sizes:
    def __init__(self, fields, modes, faces, bases, members, width, messages):
        self.F, self.M, self.C, self.B, self.E = fields, modes, faces, bases, members
        self.W, self.K = width, messages
        self.H = members // 2
        self.FP = up(fields, 2) // 2
        self.MP = up(modes, 64)
        self.BP = up(bases, 8)
        self.BQ = up(bases, 16)
        self.R = fields * self.BP
        self.RP = up(self.R, 16)
        self.Q = members // width
        self.QR = up(up(self.R, 8 * self.Q) // self.Q, 8)
        self.KW = up(messages * width, 128)
        self.S = faces * members


def filled(x, rows):
    if x.shape[0] == rows:
        return x
    return jnp.concatenate([x, jnp.zeros((rows - x.shape[0], x.shape[1]), x.dtype)], axis=0)


def put_field(z, y3, f, x):
    hi, lo = halves(filled(x, z.MP))
    lanes = slice(f * z.E, (f + 1) * z.E)
    y3[0:z.MP, lanes] = hi
    y3[z.MP:2 * z.MP, lanes] = lo
    y3[2 * z.MP:3 * z.MP, lanes] = hi


def put_face(z, u, c, lanes, hi, lo):
    for part, value in enumerate((hi, lo, hi)):
        at = (part * z.C + c) * z.BQ
        u[at:at + z.BQ, lanes] = value


def lane(z, i):
    return slice(i * z.E, (i + 1) * z.E)


def take(x, row):
    return jnp.take_along_axis(x, jnp.broadcast_to(row, x.shape), axis=1)


def low_lanes(z, rows):
    return lax.broadcasted_iota(jnp.int32, (rows, z.E), 1) < z.H


def fold(z, first, second):
    low = low_lanes(z, first.shape[0])
    second = jnp.zeros_like(first) if second is None else second
    return jnp.where(low, first, second) + pltpu.roll(jnp.where(low, second, first), z.H, 1)


def compact(z, pick, field):
    low = low_lanes(z, z.M)
    out = []
    for p in range(z.FP):
        a = take(field(2 * p), pick)
        b = take(field(2 * p + 1), pick) if 2 * p + 1 < z.F else jnp.zeros_like(a)
        out.append(jnp.where(low, a, b))
    return out


def expand(z, rank, pairs, f):
    return take(pairs(f // 2), rank + z.H * (f % 2))


def star_sum(z, start, group, turned, star, count):
    total = list(start)
    for f in range(count):
        for d in range(3):
            t = turned[d * z.M:(d + 1) * z.M, lane(z, f)]
            for i, g in enumerate(group):
                term = star[g, f, d:d + 1, :] * t
                total[i] = term if total[i] is None else total[i] + term
    return total


def star_pair(z, p, turned, star):
    group = [g for g in (2 * p, 2 * p + 1) if g < z.F]
    total = star_sum(z, [None] * len(group), group, turned, star, z.FP)
    return fold(z, total[0], total[1] if len(group) == 2 else None)


def face_sum(z, flux, g, c, t):
    total = flux[g, 0, c:c + 1, :] * t[0]
    for f in range(1, len(t)):
        total = total + flux[g, f, c:c + 1, :] * t[f]
    return total


def face_rows(z, traces, c, count):
    return [traces[c * z.BP:(c + 1) * z.BP, lane(z, f)] for f in range(count)]


def groups_of(n, size):
    return [list(range(i, min(n, i + size))) for i in range(0, n, size)]


def pack_messages(z, sent, ohs, sx, messages, picked):
    hi, lo = halves(sent[...])
    sx[0:z.R, :] = hi
    sx[z.RP:z.RP + z.R, :] = lo
    both = dot(sx[...], ohs[...])
    picked[...] = both[0:z.R, :] + both[z.RP:z.RP + z.R, :]
    for m, message in enumerate(messages):
        for q in range(z.Q):
            rows = min(z.R, (q + 1) * z.QR) - q * z.QR
            lanes = slice(q * z.W, (q + 1) * z.W)
            message[0:rows, lanes] = picked[q * z.QR:q * z.QR + rows, m * z.W:(m + 1) * z.W]
            if rows < z.QR:
                message[rows:z.QR, lanes] = jnp.zeros((z.QR - rows, z.W), F32)


def triple(rows, cols, target, wide, matrix):
    hi = matrix.astype(BF).astype(F32)
    wide[rows, 0:cols] = hi
    wide[rows, cols:2 * cols] = hi
    wide[rows, 2 * cols:3 * cols] = matrix - hi
    target[rows, :] = wide[rows, 0:3 * cols].astype(BF)


def first_kernel(z, plan, *refs):
    n = 10
    hbm, refs = refs[:n], refs[n:]
    (y, star, local, across, deriv, volume, partner, cluster, p3, square, ohs, y3, traces, sx), refs = refs[:14], refs[14:]
    messages, refs = refs[:z.K], refs[z.K:]
    projection, slots, sent, picked, picks, wide, sem = refs
    targets = (y, projection, slots, across, star, local, deriv, volume, partner, cluster)
    copies = [pltpu.make_async_copy(a, b, sem.at[i]) for i, (a, b) in enumerate(zip(hbm, targets))]
    for copy in copies:
        copy.start()
    square[...] = jnp.zeros_like(square)
    wide[...] = jnp.zeros_like(wide)
    picks[...] = jnp.full_like(picks, -1)
    upward, _ = bearings(plan)
    copies[2].wait()
    for m, (a, rises) in enumerate(upward):
        picks[0:1, m * z.W:(m + 1) * z.W] = jnp.where(rises, slots[2 * a + 1:2 * a + 2, :], slots[2 * a:2 * a + 1, :])
    ids = lax.broadcasted_iota(jnp.int32, (z.S, z.KW), 0)
    ohs[...] = jnp.where(ids == picks[0:1, :], 1.0, 0.0).astype(BF)
    copies[1].wait()
    for c in range(z.C):
        for b in range(z.B):
            square[c * z.BQ + b:c * z.BQ + b + 1, 0:z.M] = projection[b, c:c + 1, :]
    for c in range(z.C):
        rows = slice(c * z.BP, (c + 1) * z.BP)
        triple(rows, z.MP, p3, wide, square[c * z.BQ:c * z.BQ + z.BP, 0:z.MP])
    copies[0].wait()
    for f in range(z.F):
        put_field(z, y3, f, y[f * z.M:(f + 1) * z.M, :])
    traces[...] = dot(p3[...], y3[...])
    copies[3].wait()
    for c in range(z.C):
        t = face_rows(z, traces, c, z.F)
        for g in range(z.F):
            sent[g * z.BP:(g + 1) * z.BP, lane(z, c)] = face_sum(z, across, g, c, t)
    pack_messages(z, sent, ohs, sx, messages, picked)
    for copy in copies[4:]:
        copy.wait()


def set_up(z, plan, deriv, volume, square, partner, cluster, ohs, star, across, local, outs, scratch):
    s3, v3, pt, ohr, ohl, ohs_half, ohl_half, index, star_pairs, across_pairs, local_pairs = outs
    wide, block, picks = scratch
    wide[...] = jnp.zeros_like(wide)
    block[...] = jnp.zeros_like(block)
    for source, target in ((deriv, s3), (volume, v3)):
        for d in range(3):
            block[0:z.M, 0:z.M] = source[d]
            turned = jnp.transpose(block[...])
            triple(slice(d * z.M, (d + 1) * z.M), z.MP, target, wide, turned[0:z.M, 0:z.MP])
    triple(slice(0, z.M), z.C * z.BQ, pt, wide, jnp.transpose(square[...])[0:z.M, 0:z.C * z.BQ])
    _, arrival = bearings(plan)
    far = partner[...] - z.S
    moved = jnp.full_like(far, -1)
    for i in range(6):
        here = jnp.logical_and(far >= i * z.W, far < (i + 1) * z.W)
        here = jnp.logical_and(here, arrival[i] >= 0)
        moved = jnp.where(here, arrival[i] * z.W + far - i * z.W, moved)
    slots = partner[...]
    for c in range(z.C):
        ids = lax.broadcasted_iota(jnp.int32, (z.S, z.E), 0)
        ohl[:, lane(z, c)] = jnp.where(ids == slots[c:c + 1, :], 1.0, 0.0).astype(BF)
        ids = lax.broadcasted_iota(jnp.int32, (z.KW, z.E), 0)
        ohr[:, lane(z, c)] = jnp.where(ids == moved[c:c + 1, :], 1.0, 0.0).astype(BF)
    fast = cluster[...] == 0
    flags = jnp.broadcast_to(jnp.where(fast, 1.0, 0.0), (8, z.E))
    a = lax.broadcasted_iota(jnp.int32, (z.E, z.E), 0)
    b = lax.broadcasted_iota(jnp.int32, (z.E, z.E), 1)
    below = jnp.where(a <= b, 1.0, 0.0).astype(BF)
    running = dot(flags.astype(BF), below)
    count = dot(flags.astype(BF), jnp.ones((z.E, z.E), BF))
    rank = running[0:1, :].astype(jnp.int32) - 1
    held = jnp.where(fast, rank, -1)
    chosen = jnp.where(lax.broadcasted_iota(jnp.int32, (z.H, z.E), 0) == held, 1.0, 0.0).astype(BF)
    numbers = lax.broadcasted_iota(jnp.int32, (8, z.E), 1).astype(F32).astype(BF)
    listed = lax.dot_general(numbers, chosen, (((1,), (1,)), ((), ())), preferred_element_type=F32)
    picks[:, 0:z.H] = listed
    picks[:, z.H:2 * z.H] = listed
    pick = picks[0:1, :].astype(jnp.int32)
    place = lax.broadcasted_iota(jnp.int32, (1, z.E), 1)
    place = jnp.where(place < z.H, place, place - z.H)
    live = place < count[0:1, :].astype(jnp.int32)
    index[...] = jnp.zeros_like(index)
    index[0:1, :] = pick
    index[1:2, :] = jnp.maximum(rank, 0)
    index[2:3, :] = jnp.where(fast, 1, 0)
    for c in range(z.C):
        rows = slice(c * z.H, (c + 1) * z.H)
        ohs_half[rows, :] = dot(chosen, ohs[lane(z, c), :]).astype(BF)
        ohl_half[rows, :] = dot(chosen, ohl[lane(z, c), :]).astype(BF)
    for source, target in ((star, star_pairs), (across, across_pairs), (local, local_pairs)):
        low = jnp.logical_and(low_lanes(z, 1), live)
        high = jnp.logical_and(jnp.logical_not(low_lanes(z, 1)), live)
        for g in range(z.F):
            for p in range(z.FP):
                value = jnp.where(low, take(source[g, 2 * p], pick), 0.0)
                if 2 * p + 1 < z.F:
                    value = jnp.where(high, take(source[g, 2 * p + 1], pick), value)
                target[g, p] = value


def first_local_kernel(z, plan, *refs):
    deriv, volume, square, partner, cluster, ohs, star, across, local, y3, traces, sx = refs[:12]
    outs, src, refs = refs[12:23], refs[23], refs[24:]
    turned, u, gathered, *scratch = refs
    set_up(z, plan, deriv, volume, square, partner, cluster, ohs, star, across, local, outs, scratch)
    v3, pt, ohl = outs[1], outs[2], outs[4]
    turned[...] = dot(v3[...], y3[...])
    gathered[...] = dot(sx[...], ohl[...])
    for c in range(z.C):
        t = face_rows(z, traces, c, z.F)
        for g in range(z.F):
            total = gathered[g * z.BP:(g + 1) * z.BP, lane(z, c)] + gathered[z.RP + g * z.BP:z.RP + (g + 1) * z.BP, lane(z, c)]
            hi, lo = halves(filled(total + face_sum(z, local, g, c, t), z.BQ))
            put_face(z, u, c, lane(z, g), hi, lo)
    lifted = dot(pt[...], u[...])
    for group in groups_of(z.F, 3):
        start = [lifted[:, lane(z, g)] for g in group]
        for g, total in zip(group, star_sum(z, start, group, turned, star, z.F)):
            src[g * z.M:(g + 1) * z.M, :] = total


def lift_gathered(z, gathered, u, pt):
    for c in range(z.C):
        for g in range(z.F):
            hi = filled(gathered[g * z.BP:(g + 1) * z.BP, lane(z, c)], z.BQ).astype(BF)
            lo = filled(gathered[z.RP + g * z.BP:z.RP + (g + 1) * z.BP, lane(z, c)], z.BQ).astype(BF)
            put_face(z, u, c, lane(z, g), hi, lo)
    return dot(pt[...], u[...])


def local_kernel(z, last, *refs):
    y3, traces, sx, v3, pt, star, local, ohl, index, src_in, half_in = refs[:11]
    refs = refs[11:]
    if last:
        older, start, moved, refs = refs[0:2], refs[2], refs[3], refs[4:]
        src_out, weights, base, refs = refs[0], refs[1], refs[2], refs[3:]
        half_out = refs[0]
        refs = refs[1:]
    else:
        src_out, half_out, refs = refs[0], refs[1], refs[2:]
    turned, u, gathered, u_half, lifted = refs
    turned[...] = dot(v3[...], y3[...])
    gathered[...] = dot(sx[...], ohl[...])
    for c in range(z.C):
        t = face_rows(z, traces, c, z.FP)
        for p in range(z.FP):
            first = face_sum(z, local, 2 * p, c, t)
            second = face_sum(z, local, 2 * p + 1, c, t) if 2 * p + 1 < z.F else None
            hi, lo = halves(filled(fold(z, first, second), z.BQ))
            put_face(z, u_half, c, lane(z, p), hi, lo)
    lifted_half = dot(pt[...], u_half[...])
    lifted[...] = lift_gathered(z, gathered, u, pt)
    pick, rank = index[0:1, :], index[1:2, :]
    gained = compact(z, pick, lambda f: lifted[:, lane(z, f)])
    for p in range(z.FP):
        rows = slice(p * z.M, (p + 1) * z.M)
        half_out[rows, :] = half_in[rows, :] + gained[p] + lifted_half[:, lane(z, p)] + star_pair(z, p, turned, star)
    fast = index[2:3, :] > 0
    for g in range(z.F):
        rows = slice(g * z.M, (g + 1) * z.M)
        value = src_in[rows, :] + lifted[:, lane(z, g)]
        if last:
            pairs = lambda p: half_out[p * z.M:(p + 1) * z.M, :]
            src_out[rows, :] = jnp.where(fast, expand(z, rank, pairs, g), value)
            pairs = lambda p: moved[p * z.M:(p + 1) * z.M, :]
            base[rows, :] = start[rows, :] + jnp.where(fast, expand(z, rank, pairs, g), 0.0)
            sources = [x[rows, :] for x in older] + [src_in[rows, :]]
            sources = [jnp.where(fast, 0.0, x) for x in sources]
            for k in range(TERMS):
                total = None
                for step, x in zip(range(FINE_STEPS - 1, 0, -1), sources):
                    c = coefficients(step / FINE_STEPS, (step + 1) / FINE_STEPS)[k]
                    total = c * x if total is None else total + c * x
                weights[k, rows, :] = total
        else:
            src_out[rows, :] = value


def arrive(z, arrived, ohr, pt, landed, stacked, gathered, u):
    used = z.K * z.W // 128 * 128
    if used < z.KW:
        landed[:, used:z.KW] = jnp.zeros((z.R, z.KW - used), F32)
    for m in range(z.K):
        for q in range(z.Q):
            rows = min(z.R, (q + 1) * z.QR) - q * z.QR
            landed[q * z.QR:q * z.QR + rows, m * z.W:(m + 1) * z.W] = arrived[m][0:rows, q * z.W:(q + 1) * z.W]
    hi, lo = halves(landed[...])
    stacked[0:z.R, :] = hi
    stacked[z.RP:z.RP + z.R, :] = lo
    gathered[...] = dot(stacked[...], ohr[...])
    return lift_gathered(z, gathered, u, pt)


def step_kernel(z, first, *refs):
    arrived, refs = refs[:z.K], refs[z.K:]
    src_in, half_in, moved_in, s3, p3, pt, star, across, ohr, ohs, index = refs[:11]
    src_out, half, moved, y3, traces, sx = refs[11:17]
    messages, refs = refs[17:17 + z.K], refs[17 + z.K:]
    landed, stacked, gathered, u, lifted, turned, change, sent, picked = refs
    lifted[...] = arrive(z, arrived, ohr, pt, landed, stacked, gathered, u)
    for g in range(z.F):
        rows = slice(g * z.M, (g + 1) * z.M)
        src_out[rows, :] = src_in[rows, :] + lifted[:, lane(z, g)]
    if first:
        gained = compact(z, index[0:1, :], lambda f: src_out[f * z.M:(f + 1) * z.M, :])
    else:
        gained = compact(z, index[0:1, :], lambda f: lifted[:, lane(z, f)])
    row = coefficients(0.0, 1.0 / FINE_STEPS)
    for p in range(z.FP):
        rows = slice(p * z.M, (p + 1) * z.M)
        value = gained[p] if first else half_in[rows, :] + gained[p]
        half[rows, :] = value
        put_field(z, y3, p, row[TERMS - 1] * value)

    def term(i, carry):
        c = F32(row[TERMS - 2])
        for k in range(TERMS - 2):
            c = jnp.where(i == TERMS - 2 - k, F32(row[k]), c)
        turned[...] = dot(s3[...], y3[...])
        for p in range(z.FP):
            rows = slice(p * z.M, (p + 1) * z.M)
            total = c * half[rows, :] + star_pair(z, p, turned, star)
            put_field(z, y3, p, total)
            change[rows, :] = total
        return carry

    lax.fori_loop(0, TERMS - 1, term, 0)
    moved[...] = change[...] if first else moved_in[...] + change[...]
    traces[...] = dot(p3[...], y3[...])
    for pair in groups_of(z.C, 2):
        t = [face_rows(z, traces, c, z.FP) for c in pair]
        for g in range(z.F):
            total = fold(z, *[face_sum(z, across, g, c, t[i]) for i, c in enumerate(pair)])
            sent[g * z.BP:(g + 1) * z.BP, lane(z, pair[0] // 2)] = total
    pack_messages(z, sent, ohs, sx, messages, picked)


def last_kernel(z, *refs):
    arrived, refs = refs[:z.K], refs[z.K:]
    src_in, weights, base, s3, pt, star, ohr, out = refs[:8]
    landed, stacked, gathered, u, lifted, turned, y3, src = refs[8:]
    lifted[...] = arrive(z, arrived, ohr, pt, landed, stacked, gathered, u)
    row = coefficients(0.0, 1.0 / FINE_STEPS)
    for g in range(z.F):
        rows = slice(g * z.M, (g + 1) * z.M)
        value = src_in[rows, :] + lifted[:, lane(z, g)]
        src[rows, :] = value
        put_field(z, y3, g, weights[TERMS - 1, rows, :] + row[TERMS - 1] * value)

    def term(i, carry):
        c = F32(row[TERMS - 2])
        for k in range(TERMS - 2):
            c = jnp.where(i == TERMS - 2 - k, F32(row[k]), c)
        turned[...] = dot(s3[...], y3[...])
        for group in groups_of(z.F, 3):
            start = [weights[TERMS - 2 - i, g * z.M:(g + 1) * z.M, :] + c * src[g * z.M:(g + 1) * z.M, :] for g in group]
            for g, total in zip(group, star_sum(z, start, group, turned, star, z.F)):
                put_field(z, y3, g, total)
                out[g * z.M:(g + 1) * z.M, :] = total
        return carry

    lax.fori_loop(0, TERMS - 1, term, 0)
    out[...] = out[...] + base[...]


def call(kernel, outs, scratch, *args, remote=False):
    place = pl.BlockSpec(memory_space=pltpu.HBM if remote else pltpu.VMEM)
    if remote:
        args = [pltpu.with_memory_space_constraint(x, pltpu.HBM) for x in args]
    vmem = pl.BlockSpec(memory_space=pltpu.VMEM)
    return pl.pallas_call(
        kernel,
        out_shape=[jax.ShapeDtypeStruct(*o) for o in outs],
        in_specs=[place] * len(args),
        out_specs=[vmem] * len(outs),
        scratch_shapes=[pltpu.VMEM(*o) if isinstance(o, tuple) else o for o in scratch],
        compiler_params=pltpu.CompilerParams(vmem_limit_bytes=24 << 20),
        cost_estimate=pl.CostEstimate(flops=1 << 30, bytes_accessed=2 << 20, transcendentals=0),
    )(*args)


def body(
    final_adjoint,
    star_mats,
    deriv_stiff,
    volume_stiffness,
    face_projection,
    flux_local,
    flux_across,
    cluster,
    partner,
    send_slots,
):
    fields, modes, members = final_adjoint.shape
    faces, bases, _ = face_projection.shape
    plan = matchings()
    width = send_slots.shape[1]
    z = Sizes(fields, modes, faces, bases, members, width, len(plan))

    full, half = ((fields * modes, members), F32), ((z.FP * modes, members), F32)
    y3, y3_half = ((3 * z.MP, fields * members), BF), ((3 * z.MP, z.FP * members), BF)
    traces, traces_half = ((faces * z.BP, fields * members), F32), ((faces * z.BP, z.FP * members), F32)
    turned, turned_half = ((3 * modes, fields * members), F32), ((3 * modes, z.FP * members), F32)
    u, u_half = ((3 * faces * z.BQ, fields * members), BF), ((3 * faces * z.BQ, z.FP * members), BF)
    gathered, lifted = ((2 * z.RP, z.S), F32), ((modes, fields * members), F32)
    landed, stacked = ((z.R, z.KW), F32), ((2 * z.RP, z.KW), BF)
    sx, sx_half = ((2 * z.RP, z.S), BF), ((2 * z.RP, z.S // 2), BF)
    sent, sent_half, picked = ((z.R, z.S), F32), ((z.R, z.S // 2), F32), ((z.R, z.KW), F32)
    messages_out = [((z.QR, members), F32)] * z.K
    wide = ((3 * modes, up(3 * max(z.MP, faces * z.BQ), 128)), F32)
    pairs = lambda n: ((fields, z.FP, n, members), F32)

    def trade(messages):
        return [lax.ppermute(m, axis, links) for m, (axis, links, _) in zip(messages, plan)]

    star = jnp.transpose(star_mats, (1, 2, 0, 3))
    local = jnp.transpose(flux_local, (1, 2, 0, 3))
    across = jnp.transpose(flux_across, (1, 2, 0, 3))
    args = [
        final_adjoint.reshape(fields * modes, members), jnp.transpose(face_projection, (1, 0, 2)), send_slots, across,
        star, local, deriv_stiff, volume_stiffness, partner, cluster.reshape(1, members),
    ]
    like = lambda x: (x.shape, x.dtype)
    (start, star, local, across, deriv, volume, partner, cluster, p3, square, ohs, y3v, tr, sxv, *messages) = call(
        functools.partial(first_kernel, z, plan),
        [like(args[i]) for i in (0, 4, 5, 3, 6, 7, 8, 9)]
        + [((faces * z.BP, 3 * z.MP), BF), ((128, 128), F32), ((z.S, z.KW), BF), y3, traces, sx] + messages_out,
        [like(args[1]), like(args[2]), sent, picked, ((8, z.KW), jnp.int32), wide, pltpu.SemaphoreType.DMA((len(args),))],
        *args, remote=True,
    )
    arrived = trade(messages)
    s3, v3, pt, ohr, ohl, ohs_half, ohl_half, index, star_pairs, across_pairs, local_pairs, src = call(
        functools.partial(first_local_kernel, z, plan),
        [((3 * modes, 3 * z.MP), BF), ((3 * modes, 3 * z.MP), BF), ((modes, 3 * faces * z.BQ), BF), ((z.KW, z.S), BF),
         ((z.S, z.S), BF), ((z.S // 2, z.KW), BF), ((z.S // 2, z.S), BF), ((8, members), jnp.int32),
         pairs(3), pairs(faces), pairs(faces), full],
        [turned, u, gathered, wide, ((128, 128), F32), ((8, members), F32)],
        deriv, volume, square, partner, cluster, ohs, star, across, local, y3v, tr, sxv,
    )
    half_src = moved = jnp.zeros((8, members), F32)
    sources = []
    for step in range(FINE_STEPS - 1, 0, -1):
        src, half_src, moved, y3v, tr, sxv, *messages = call(
            functools.partial(step_kernel, z, step == FINE_STEPS - 1),
            [full, half, half, y3_half, traces_half, sx_half] + messages_out,
            [landed, stacked, gathered, u, lifted, turned_half, half, sent_half, picked],
            *arrived, src, half_src, moved, s3, p3, pt, star_pairs, across_pairs, ohr, ohs_half, index,
        )
        arrived = trade(messages)
        sources.append(src)
        last = step == 1
        local_args = [y3v, tr, sxv, v3, pt, star_pairs, local_pairs, ohl_half, index, src, half_src]
        local_scratch = [turned_half, u, gathered, u_half, lifted]
        if last:
            src, weights, base, _ = call(
                functools.partial(local_kernel, z, True), [full, ((TERMS,) + full[0], F32), full, half], local_scratch,
                *local_args, *sources[:2], start, moved,
            )
        else:
            src, half_src = call(functools.partial(local_kernel, z, False), [full, half], local_scratch, *local_args)
    (out,) = call(
        functools.partial(last_kernel, z), [full],
        [landed, stacked, gathered, u, lifted, turned, y3, full],
        *arrived, src, weights, base, s3, pt, star, ohr,
    )
    return out.reshape(fields, modes, members)


def solution(mesh):
    in_specs = (
        P(None, None, ("gx", "gy", "gz")),
        P(None, None, None, ("gx", "gy", "gz")),
        P(),
        P(),
        P(),
        P(None, None, None, ("gx", "gy", "gz")),
        P(None, None, None, ("gx", "gy", "gz")),
        P(("gx", "gy", "gz")),
        P(None, ("gx", "gy", "gz")),
        P(None, ("gx", "gy", "gz")),
    )
    out_specs = P(None, None, ("gx", "gy", "gz"))
    return jax.shard_map(body, mesh=mesh, in_specs=in_specs, out_specs=out_specs, check_vma=False)
```

```python
import functools
import math

import jax
import jax.numpy as jnp
from jax import lax
from jax.experimental import pallas as pl
from jax.experimental.pallas import tpu as pltpu
from jax.sharding import PartitionSpec as P

TERMS = 6
FINE_STEPS = 4
BF = jnp.bfloat16
F32 = jnp.float32


def up(n, unit):
    return -(-n // unit) * unit


AXES = ("gx", "gy", "gz")


def matchings():
    plan = []
    for axis in AXES:
        size = lax.axis_size(axis)
        for first in (0, 1):
            links = [(i, i + 1) for i in range(first, size - 1, 2)]
            if not links:
                continue
            if first == 1 and size % 2 == 0:
                links.append((size - 1, 0))
            plan.append((axis, [q for i, j in links for q in ((i, j), (j, i))], first))
    return plan


def bearings(plan):
    upward, block = [], [jnp.int32(-1)] * 6
    for number, (axis, _, first) in enumerate(plan):
        a, place, size = AXES.index(axis), lax.axis_index(axis), lax.axis_size(axis)
        rises = lax.rem(place, 2) == first
        upward.append((a, rises))
        for side in (0, 1):
            inside = (place > 0) if side == 0 else (place < size - 1)
            used = jnp.logical_and(rises if side == 1 else jnp.logical_not(rises), inside)
            block[2 * a + side] = jnp.where(used, number, block[2 * a + side])
    return upward, block


def coefficients(lower, upper):
    return [(upper ** (k + 1) - lower ** (k + 1)) / math.factorial(k + 1) for k in range(TERMS)]


def halves(x):
    hi = x.astype(BF)
    return hi, (x - hi.astype(F32)).astype(BF)


def dot(a, b):
    return jnp.dot(a, b, preferred_element_type=F32)


class Sizes:
    def __init__(self, fields, modes, faces, bases, members, width, messages):
        self.F, self.M, self.C, self.B, self.E = fields, modes, faces, bases, members
        self.W, self.K = width, messages
        self.H = members // 2
        self.FP = up(fields, 2) // 2
        self.MP = up(modes, 64)
        self.BP = up(bases, 8)
        self.BQ = up(bases, 16)
        self.R = fields * self.BP
        self.RP = up(self.R, 16)
        self.Q = members // width
        self.QR = up(up(self.R, 8 * self.Q) // self.Q, 8)
        self.KW = up(messages * width, 128)
        self.S = faces * members


def filled(x, rows):
    if x.shape[0] == rows:
        return x
    return jnp.concatenate([x, jnp.zeros((rows - x.shape[0], x.shape[1]), x.dtype)], axis=0)


def put_field(z, y3, f, x):
    hi, lo = halves(filled(x, z.MP))
    lanes = slice(f * z.E, (f + 1) * z.E)
    y3[0:z.MP, lanes] = hi
    y3[z.MP:2 * z.MP, lanes] = lo
    y3[2 * z.MP:3 * z.MP, lanes] = hi


def put_face(z, u, c, lanes, hi, lo):
    for part, value in enumerate((hi, lo, hi)):
        at = (part * z.C + c) * z.BQ
        u[at:at + z.BQ, lanes] = value


def lift(z, pt, u):
    return dot(pt[...], u[...])


def lane(z, i):
    return slice(i * z.E, (i + 1) * z.E)


def take(x, row):
    return jnp.take_along_axis(x, jnp.broadcast_to(row, x.shape), axis=1)


def low_lanes(z, rows):
    return lax.broadcasted_iota(jnp.int32, (rows, z.E), 1) < z.H


def balanced(z, out, matrix, y3):
    rows, lanes = matrix.shape[0], out.shape[1]
    even = lanes // (2 * z.E) * 2 * z.E
    out[0:rows, 0:even] = dot(matrix[...], y3[:, 0:even])
    if even < lanes:
        cut = up(rows // 2, 16)
        out[0:cut, even:lanes] = dot(matrix[0:cut, :], y3[:, even:lanes])
        out[cut:rows, even:lanes] = dot(matrix[cut:rows, :], y3[:, even:lanes])


def fold(z, first, second):
    low = low_lanes(z, first.shape[0])
    second = jnp.zeros_like(first) if second is None else second
    return jnp.where(low, first, second) + pltpu.roll(jnp.where(low, second, first), z.H, 1)


def compact(z, pick, field):
    low = low_lanes(z, z.M)
    out = []
    for p in range(z.FP):
        a = take(field(2 * p), pick)
        b = take(field(2 * p + 1), pick) if 2 * p + 1 < z.F else jnp.zeros_like(a)
        out.append(jnp.where(low, a, b))
    return out


def expand(z, rank, pairs, f):
    return take(pairs(f // 2), rank + z.H * (f % 2))


def star_sum(z, start, group, turned, star, count):
    total = list(start)
    for f in range(count):
        for d in range(3):
            t = turned[d * z.M:(d + 1) * z.M, lane(z, f)]
            for i, g in enumerate(group):
                term = star[g, f, d:d + 1, :] * t
                total[i] = term if total[i] is None else total[i] + term
    return total


def mark(ref, at, parts):
    for i, x in enumerate(parts):
        ref[pl.ds(pl.multiple_of(at, 8), 8), i * x.shape[1]:(i + 1) * x.shape[1]] = x[0:8, :]


def star_pair(z, p, turned, star):
    group = [g for g in (2 * p, 2 * p + 1) if g < z.F]
    total = star_sum(z, [None] * len(group), group, turned, star, z.FP)
    return fold(z, total[0], total[1] if len(group) == 2 else None)


def face_sum(z, flux, g, c, t):
    total = flux[g, 0, c:c + 1, :] * t[0]
    for f in range(1, len(t)):
        total = total + flux[g, f, c:c + 1, :] * t[f]
    return total


def face_rows(z, traces, c, count):
    return [traces[c * z.BP:(c + 1) * z.BP, lane(z, f)] for f in range(count)]


def groups_of(n, size):
    return [list(range(i, min(n, i + size))) for i in range(0, n, size)]


def regroup(z, base, part):
    group = lax.broadcasted_iota(jnp.int32, (z.QR, z.E), 1)
    out = None
    for q in range(z.Q):
        shift = (q - base) % z.Q * z.W
        x = part(q)
        x = pltpu.roll(x, shift, 1) if shift else x
        out = x if out is None else jnp.where(group >= q * z.W, x, out)
    return out


def ungroup(z, messages, q):
    group = lax.broadcasted_iota(jnp.int32, (z.QR, z.E), 1)
    out = None
    for m, message in enumerate(messages):
        shift = (m - q) % z.Q * z.W
        x = message[...]
        x = pltpu.roll(x, shift, 1) if shift else x
        out = x if out is None else jnp.where(group >= m * z.W, x, out)
    if len(messages) < z.Q:
        out = jnp.where(group < len(messages) * z.W, out, 0.0)
    return out


def pack_messages(z, sent, ohs, sx, messages, picked):
    hi, lo = halves(sent[...])
    sx[0:z.R, :] = hi
    sx[z.RP:z.RP + z.R, :] = lo
    both = dot(sx[...], ohs[...])
    picked[...] = both[0:z.R, :] + both[z.RP:z.RP + z.R, :]
    for m, message in enumerate(messages):
        home = lane(z, m // z.Q)
        message[...] = regroup(z, m % z.Q, lambda q: filled(picked[q * z.QR:min(z.R, (q + 1) * z.QR), home], z.QR))


def triple(rows, cols, target, wide, matrix):
    hi = matrix.astype(BF).astype(F32)
    wide[rows, 0:cols] = hi
    wide[rows, cols:2 * cols] = hi
    wide[rows, 2 * cols:3 * cols] = matrix - hi
    target[rows, :] = wide[rows, 0:3 * cols].astype(BF)


def first_kernel(z, plan, *refs):
    n = 10
    hbm, refs = refs[:n], refs[n:]
    (y, star, local, across, deriv, volume, partner, cluster, p3, square, ohs, y3, traces, sx), refs = refs[:14], refs[14:]
    messages, refs = refs[:z.K], refs[z.K:]
    projection, slots, sent, picked, picks, wide, sem = refs
    targets = (y, projection, slots, across, star, local, deriv, volume, partner, cluster)
    copies = [pltpu.make_async_copy(a, b, sem.at[i]) for i, (a, b) in enumerate(zip(hbm, targets))]
    for i in (2, 1, 0, 3, *range(4, n)):
        copies[i].start()
    square[...] = jnp.zeros_like(square)
    wide[...] = jnp.zeros_like(wide)
    picks[...] = jnp.full_like(picks, -1)
    upward, _ = bearings(plan)
    copies[2].wait()
    for m, (a, rises) in enumerate(upward):
        picks[0:1, m * z.W:(m + 1) * z.W] = jnp.where(rises, slots[2 * a + 1:2 * a + 2, :], slots[2 * a:2 * a + 1, :])
    ids = lax.broadcasted_iota(jnp.int32, (z.S, z.KW), 0)
    ohs[...] = jnp.where(ids == picks[0:1, :], 1.0, 0.0).astype(BF)
    copies[1].wait()
    for c in range(z.C):
        for b in range(z.B):
            square[c * z.BQ + b:c * z.BQ + b + 1, 0:z.M] = projection[b, c:c + 1, :]
    for c in range(z.C):
        rows = slice(c * z.BP, (c + 1) * z.BP)
        triple(rows, z.MP, p3, wide, square[c * z.BQ:c * z.BQ + z.BP, 0:z.MP])
    copies[0].wait()
    for f in range(z.F):
        put_field(z, y3, f, y[f * z.M:(f + 1) * z.M, :])
    traces[...] = dot(p3[...], y3[...])
    copies[3].wait()
    for c in range(z.C):
        t = face_rows(z, traces, c, z.F)
        for g in range(z.F):
            sent[g * z.BP:(g + 1) * z.BP, lane(z, c)] = face_sum(z, across, g, c, t)
    pack_messages(z, sent, ohs, sx, messages, picked)
    for copy in copies[4:]:
        copy.wait()


def set_up(z, plan, deriv, volume, square, partner, cluster, ohs, star, across, local, outs, scratch):
    s3, v3, pt, ohr, ohl, ohs_half, ohl_half, index, star_pairs, across_pairs, local_pairs = outs
    wide, block, picks = scratch
    wide[...] = jnp.zeros_like(wide)
    block[...] = jnp.zeros_like(block)
    for source, target in ((deriv, s3), (volume, v3)):
        for d in range(3):
            block[0:z.M, 0:z.M] = source[d]
            turned = jnp.transpose(block[...])
            triple(slice(d * z.M, (d + 1) * z.M), z.MP, target, wide, turned[0:z.M, 0:z.MP])
    triple(slice(0, z.M), z.C * z.BQ, pt, wide, jnp.transpose(square[...])[0:z.M, 0:z.C * z.BQ])
    _, arrival = bearings(plan)
    far = partner[...] - z.S
    moved = jnp.full_like(far, -1)
    for i in range(6):
        here = jnp.logical_and(far >= i * z.W, far < (i + 1) * z.W)
        here = jnp.logical_and(here, arrival[i] >= 0)
        moved = jnp.where(here, arrival[i] * z.W + far - i * z.W, moved)
    slots = partner[...]
    for c in range(z.C):
        ids = lax.broadcasted_iota(jnp.int32, (z.S, z.E), 0)
        ohl[:, lane(z, c)] = jnp.where(ids == slots[c:c + 1, :], 1.0, 0.0).astype(BF)
        ids = lax.broadcasted_iota(jnp.int32, (z.KW, z.E), 0)
        ohr[:, lane(z, c)] = jnp.where(ids == moved[c:c + 1, :], 1.0, 0.0).astype(BF)
    fast = cluster[...] == 0
    flags = jnp.broadcast_to(jnp.where(fast, 1.0, 0.0), (8, z.E))
    a = lax.broadcasted_iota(jnp.int32, (z.E, z.E), 0)
    b = lax.broadcasted_iota(jnp.int32, (z.E, z.E), 1)
    below = jnp.where(a <= b, 1.0, 0.0).astype(BF)
    running = dot(flags.astype(BF), below)
    count = dot(flags.astype(BF), jnp.ones((z.E, z.E), BF))
    rank = running[0:1, :].astype(jnp.int32) - 1
    held = jnp.where(fast, rank, -1)
    chosen = jnp.where(lax.broadcasted_iota(jnp.int32, (z.H, z.E), 0) == held, 1.0, 0.0).astype(BF)
    numbers = lax.broadcasted_iota(jnp.int32, (8, z.E), 1).astype(F32).astype(BF)
    listed = lax.dot_general(numbers, chosen, (((1,), (1,)), ((), ())), preferred_element_type=F32)
    picks[:, 0:z.H] = listed
    picks[:, z.H:2 * z.H] = listed
    pick = picks[0:1, :].astype(jnp.int32)
    place = lax.broadcasted_iota(jnp.int32, (1, z.E), 1)
    place = jnp.where(place < z.H, place, place - z.H)
    live = place < count[0:1, :].astype(jnp.int32)
    index[...] = jnp.zeros_like(index)
    index[0:1, :] = pick
    index[1:2, :] = jnp.maximum(rank, 0)
    index[2:3, :] = jnp.where(fast, 1, 0)
    for c in range(z.C):
        rows = slice(c * z.H, (c + 1) * z.H)
        ohs_half[rows, :] = dot(chosen, ohs[lane(z, c), :]).astype(BF)
        ohl_half[rows, :] = dot(chosen, ohl[lane(z, c), :]).astype(BF)
    for source, target in ((star, star_pairs), (across, across_pairs), (local, local_pairs)):
        low = jnp.logical_and(low_lanes(z, 1), live)
        high = jnp.logical_and(jnp.logical_not(low_lanes(z, 1)), live)
        for g in range(z.F):
            for p in range(z.FP):
                value = jnp.where(low, take(source[g, 2 * p], pick), 0.0)
                if 2 * p + 1 < z.F:
                    value = jnp.where(high, take(source[g, 2 * p + 1], pick), value)
                target[g, p] = value


def first_local_kernel(z, plan, *refs):
    deriv, volume, square, partner, cluster, ohs, star, across, local, y3, traces, sx = refs[:12]
    outs, src, refs = refs[12:23], refs[23], refs[24:]
    turned, u, gathered, *scratch = refs
    set_up(z, plan, deriv, volume, square, partner, cluster, ohs, star, across, local, outs, scratch)
    v3, pt, ohl = outs[1], outs[2], outs[4]
    turned[...] = dot(v3[...], y3[...])
    gathered[...] = dot(sx[...], ohl[...])
    for c in range(z.C):
        t = face_rows(z, traces, c, z.F)
        for g in range(z.F):
            total = gathered[g * z.BP:(g + 1) * z.BP, lane(z, c)] + gathered[z.RP + g * z.BP:z.RP + (g + 1) * z.BP, lane(z, c)]
            hi, lo = halves(filled(total + face_sum(z, local, g, c, t), z.BQ))
            put_face(z, u, c, lane(z, g), hi, lo)
    lifted = lift(z, pt, u)
    for group in groups_of(z.F, 3):
        start = [lifted[:, lane(z, g)] for g in group]
        for g, total in zip(group, star_sum(z, start, group, turned, star, z.F)):
            src[g * z.M:(g + 1) * z.M, :] = total


def lift_gathered(z, gathered, u, pt):
    for c in range(z.C):
        for g in range(z.F):
            hi = filled(gathered[g * z.BP:(g + 1) * z.BP, lane(z, c)], z.BQ).astype(BF)
            lo = filled(gathered[z.RP + g * z.BP:z.RP + (g + 1) * z.BP, lane(z, c)], z.BQ).astype(BF)
            put_face(z, u, c, lane(z, g), hi, lo)
    return lift(z, pt, u)


def local_kernel(z, last, *refs):
    y3, traces, sx, v3, pt, star, local, ohl, index, src_in, half_in = refs[:11]
    refs = refs[11:]
    if last:
        older, start, moved, refs = refs[0:2], refs[2], refs[3], refs[4:]
        src_out, weights, base, refs = refs[0], refs[1], refs[2], refs[3:]
        half_out = refs[0]
        refs = refs[1:]
    else:
        src_out, half_out, refs = refs[0], refs[1], refs[2:]
    turned, u, gathered, u_half, lifted = refs
    turned[...] = dot(v3[...], y3[...])
    gathered[...] = dot(sx[...], ohl[...])
    for c in range(z.C):
        t = face_rows(z, traces, c, z.FP)
        for p in range(z.FP):
            first = face_sum(z, local, 2 * p, c, t)
            second = face_sum(z, local, 2 * p + 1, c, t) if 2 * p + 1 < z.F else None
            hi, lo = halves(filled(fold(z, first, second), z.BQ))
            put_face(z, u_half, c, lane(z, p), hi, lo)
    lifted_half = lift(z, pt, u_half)
    lifted[...] = lift_gathered(z, gathered, u, pt)
    pick, rank = index[0:1, :], index[1:2, :]
    gained = compact(z, pick, lambda f: lifted[:, lane(z, f)])
    for p in range(z.FP):
        rows = slice(p * z.M, (p + 1) * z.M)
        half_out[rows, :] = half_in[rows, :] + gained[p] + lifted_half[:, lane(z, p)] + star_pair(z, p, turned, star)
    fast = index[2:3, :] > 0
    for g in range(z.F):
        rows = slice(g * z.M, (g + 1) * z.M)
        value = src_in[rows, :] + lifted[:, lane(z, g)]
        if last:
            pairs = lambda p: half_out[p * z.M:(p + 1) * z.M, :]
            src_out[rows, :] = jnp.where(fast, expand(z, rank, pairs, g), value)
            pairs = lambda p: moved[p * z.M:(p + 1) * z.M, :]
            base[rows, :] = start[rows, :] + jnp.where(fast, expand(z, rank, pairs, g), 0.0)
            sources = [x[rows, :] for x in older] + [src_in[rows, :]]
            sources = [jnp.where(fast, 0.0, x) for x in sources]
            for k in range(TERMS):
                total = None
                for step, x in zip(range(FINE_STEPS - 1, 0, -1), sources):
                    c = coefficients(step / FINE_STEPS, (step + 1) / FINE_STEPS)[k]
                    total = c * x if total is None else total + c * x
                weights[k, rows, :] = total
        else:
            src_out[rows, :] = value


def arrive(z, arrived, ohr, pt, landed, stacked, gathered, u):
    for i, group in enumerate(groups_of(z.K, z.Q)):
        for q in range(z.Q):
            rows = min(z.R, (q + 1) * z.QR) - q * z.QR
            landed[q * z.QR:q * z.QR + rows, lane(z, i)] = ungroup(z, [arrived[m] for m in group], q)[0:rows, :]
    hi, lo = halves(landed[...])
    stacked[0:z.R, :] = hi
    stacked[z.RP:z.RP + z.R, :] = lo
    gathered[...] = dot(stacked[...], ohr[...])
    return lift_gathered(z, gathered, u, pt)


def step_kernel(z, first, *refs):
    arrived, refs = refs[:z.K], refs[z.K:]
    src_in, half_in, moved_in, s3, p3, pt, star, across, ohr, ohs, index = refs[:11]
    src_out, half, moved, y3, traces, sx = refs[11:17]
    messages, refs = refs[17:17 + z.K], refs[17 + z.K:]
    landed, stacked, gathered, u, lifted, turned, change, sent, picked = refs
    lifted[...] = arrive(z, arrived, ohr, pt, landed, stacked, gathered, u)
    for g in range(z.F):
        rows = slice(g * z.M, (g + 1) * z.M)
        src_out[rows, :] = src_in[rows, :] + lifted[:, lane(z, g)]
    if first:
        gained = compact(z, index[0:1, :], lambda f: src_out[f * z.M:(f + 1) * z.M, :])
    else:
        gained = compact(z, index[0:1, :], lambda f: lifted[:, lane(z, f)])
    row = coefficients(0.0, 1.0 / FINE_STEPS)
    for p in range(z.FP):
        rows = slice(p * z.M, (p + 1) * z.M)
        value = gained[p] if first else half_in[rows, :] + gained[p]
        half[rows, :] = value
        put_field(z, y3, p, row[TERMS - 1] * value)

    def term(i, carry):
        c = F32(row[TERMS - 2])
        for k in range(TERMS - 2):
            c = jnp.where(i == TERMS - 2 - k, F32(row[k]), c)
        balanced(z, turned, s3, y3)
        for p in range(z.FP):
            rows = slice(p * z.M, (p + 1) * z.M)
            total = c * half[rows, :] + star_pair(z, p, turned, star)
            put_field(z, y3, p, total)
            change[rows, :] = total
        return carry

    lax.fori_loop(0, TERMS - 1, term, 0)
    moved[...] = change[...] if first else moved_in[...] + change[...]
    traces[...] = dot(p3[...], y3[...])
    for pair in groups_of(z.C, 2):
        t = [face_rows(z, traces, c, z.FP) for c in pair]
        for g in range(z.F):
            total = fold(z, *[face_sum(z, across, g, c, t[i]) for i, c in enumerate(pair)])
            sent[g * z.BP:(g + 1) * z.BP, lane(z, pair[0] // 2)] = total
    pack_messages(z, sent, ohs, sx, messages, picked)


def last_kernel(z, *refs):
    arrived, refs = refs[:z.K], refs[z.K:]
    src_in, weights, base, s3, pt, star, ohr, out = refs[:8]
    landed, stacked, gathered, u, lifted, turned, y3, src = refs[8:]
    lifted[...] = arrive(z, arrived, ohr, pt, landed, stacked, gathered, u)
    row = coefficients(0.0, 1.0 / FINE_STEPS)
    for g in range(z.F):
        rows = slice(g * z.M, (g + 1) * z.M)
        value = src_in[rows, :] + lifted[:, lane(z, g)]
        src[rows, :] = value
        put_field(z, y3, g, weights[TERMS - 1, rows, :] + row[TERMS - 1] * value)

    def term(i, carry):
        c = F32(row[TERMS - 2])
        for k in range(TERMS - 2):
            c = jnp.where(i == TERMS - 2 - k, F32(row[k]), c)
        turned[0:3 * z.M, :] = dot(s3[...], y3[...])
        for group in groups_of(z.F, 2):
            start = [weights[TERMS - 2 - i, g * z.M:(g + 1) * z.M, :] + c * src[g * z.M:(g + 1) * z.M, :] for g in group]
            sums = star_sum(z, start, group, turned, star, z.F)
            mark(turned, 3 * z.M + 8 * i, sums)
            for g, total in zip(group, sums):
                put_field(z, y3, g, total)
                out[g * z.M:(g + 1) * z.M, :] = total
        return carry

    lax.fori_loop(0, TERMS - 1, term, 0)
    out[...] = out[...] + base[...]


def call(kernel, outs, scratch, *args, remote=False):
    place = pl.BlockSpec(memory_space=pltpu.HBM if remote else pltpu.VMEM)
    if remote:
        args = [pltpu.with_memory_space_constraint(x, pltpu.HBM) for x in args]
    vmem = pl.BlockSpec(memory_space=pltpu.VMEM)
    return pl.pallas_call(
        kernel,
        out_shape=[jax.ShapeDtypeStruct(*o) for o in outs],
        in_specs=[place] * len(args),
        out_specs=[vmem] * len(outs),
        scratch_shapes=[pltpu.VMEM(*o) if isinstance(o, tuple) else o for o in scratch],
        compiler_params=pltpu.CompilerParams(vmem_limit_bytes=24 << 20),
        cost_estimate=pl.CostEstimate(flops=1 << 30, bytes_accessed=2 << 20, transcendentals=0),
    )(*args)


def body(
    final_adjoint,
    star_mats,
    deriv_stiff,
    volume_stiffness,
    face_projection,
    flux_local,
    flux_across,
    cluster,
    partner,
    send_slots,
):
    fields, modes, members = final_adjoint.shape
    faces, bases, _ = face_projection.shape
    plan = matchings()
    width = send_slots.shape[1]
    z = Sizes(fields, modes, faces, bases, members, width, len(plan))

    full, half = ((fields * modes, members), F32), ((z.FP * modes, members), F32)
    y3, y3_half = ((3 * z.MP, fields * members), BF), ((3 * z.MP, z.FP * members), BF)
    traces, traces_half = ((faces * z.BP, fields * members), F32), ((faces * z.BP, z.FP * members), F32)
    turned, turned_half = ((3 * modes, fields * members), F32), ((3 * modes, z.FP * members), F32)
    marked = lambda o: ((o[0][0] + 8 * (TERMS - 1), o[0][1]), o[1])
    u, u_half = ((3 * faces * z.BQ, fields * members), BF), ((3 * faces * z.BQ, z.FP * members), BF)
    gathered, lifted = ((2 * z.RP, z.S), F32), ((modes, fields * members), F32)
    landed, stacked = ((z.R, z.KW), F32), ((2 * z.RP, z.KW), BF)
    sx, sx_half = ((2 * z.RP, z.S), BF), ((2 * z.RP, z.S // 2), BF)
    sent, sent_half, picked = ((z.R, z.S), F32), ((z.R, z.S // 2), F32), ((z.R, z.KW), F32)
    messages_out = [((z.QR, members), F32)] * z.K
    wide = ((3 * modes, up(3 * max(z.MP, faces * z.BQ), 128)), F32)
    pairs = lambda n: ((fields, z.FP, n, members), F32)

    def trade(messages):
        return [lax.ppermute(m, axis, links) for m, (axis, links, _) in zip(messages, plan)]

    star = jnp.transpose(star_mats, (1, 2, 0, 3))
    local = jnp.transpose(flux_local, (1, 2, 0, 3))
    across = jnp.transpose(flux_across, (1, 2, 0, 3))
    args = [
        final_adjoint.reshape(fields * modes, members), jnp.transpose(face_projection, (1, 0, 2)), send_slots, across,
        star, local, deriv_stiff, volume_stiffness, partner, cluster.reshape(1, members),
    ]
    like = lambda x: (x.shape, x.dtype)
    (start, star, local, across, deriv, volume, partner, cluster, p3, square, ohs, y3v, tr, sxv, *messages) = call(
        functools.partial(first_kernel, z, plan),
        [like(args[i]) for i in (0, 4, 5, 3, 6, 7, 8, 9)]
        + [((faces * z.BP, 3 * z.MP), BF), ((128, 128), F32), ((z.S, z.KW), BF), y3, traces, sx] + messages_out,
        [like(args[1]), like(args[2]), sent, picked, ((8, z.KW), jnp.int32), wide, pltpu.SemaphoreType.DMA((len(args),))],
        *args, remote=True,
    )
    arrived = trade(messages)
    s3, v3, pt, ohr, ohl, ohs_half, ohl_half, index, star_pairs, across_pairs, local_pairs, src = call(
        functools.partial(first_local_kernel, z, plan),
        [((3 * modes, 3 * z.MP), BF), ((3 * modes, 3 * z.MP), BF), ((modes, 3 * faces * z.BQ), BF), ((z.KW, z.S), BF),
         ((z.S, z.S), BF), ((z.S // 2, z.KW), BF), ((z.S // 2, z.S), BF), ((8, members), jnp.int32),
         pairs(3), pairs(faces), pairs(faces), full],
        [turned, u, gathered, wide, ((128, 128), F32), ((8, members), F32)],
        deriv, volume, square, partner, cluster, ohs, star, across, local, y3v, tr, sxv,
    )
    half_src = moved = jnp.zeros((8, members), F32)
    sources = []
    for step in range(FINE_STEPS - 1, 0, -1):
        src, half_src, moved, y3v, tr, sxv, *messages = call(
            functools.partial(step_kernel, z, step == FINE_STEPS - 1),
            [full, half, half, y3_half, traces_half, sx_half] + messages_out,
            [landed, stacked, gathered, u, lifted, turned_half, half, sent_half, picked],
            *arrived, src, half_src, moved, s3, p3, pt, star_pairs, across_pairs, ohr, ohs_half, index,
        )
        arrived = trade(messages)
        sources.append(src)
        last = step == 1
        local_args = [y3v, tr, sxv, v3, pt, star_pairs, local_pairs, ohl_half, index, src, half_src]
        local_scratch = [turned_half, u, gathered, u_half, lifted]
        if last:
            src, weights, base, _ = call(
                functools.partial(local_kernel, z, True), [full, ((TERMS,) + full[0], F32), full, half], local_scratch,
                *local_args, *sources[:2], start, moved,
            )
        else:
            src, half_src = call(functools.partial(local_kernel, z, False), [full, half], local_scratch, *local_args)
    (out,) = call(
        functools.partial(last_kernel, z), [full],
        [landed, stacked, gathered, u, lifted, marked(turned), y3, full],
        *arrived, src, weights, base, s3, pt, star, ohr,
    )
    return out.reshape(fields, modes, members)


def solution(mesh):
    in_specs = (
        P(None, None, ("gx", "gy", "gz")),
        P(None, None, None, ("gx", "gy", "gz")),
        P(),
        P(),
        P(),
        P(None, None, None, ("gx", "gy", "gz")),
        P(None, None, None, ("gx", "gy", "gz")),
        P(("gx", "gy", "gz")),
        P(None, ("gx", "gy", "gz")),
        P(None, ("gx", "gy", "gz")),
    )
    out_specs = P(None, None, ("gx", "gy", "gz"))
    return jax.shard_map(body, mesh=mesh, in_specs=in_specs, out_specs=out_specs, check_vma=False)
```

```python
import functools
import math

import jax
import jax.numpy as jnp
from jax import lax
from jax.experimental import pallas as pl
from jax.experimental.pallas import tpu as pltpu
from jax.sharding import PartitionSpec as P

TERMS = 6
FINE_STEPS = 4
BF = jnp.bfloat16
F32 = jnp.float32


def up(n, unit):
    return -(-n // unit) * unit


AXES = ("gx", "gy", "gz")
ORDER = (("gx", 1), ("gx", 0), ("gz", 1), ("gy", 1), ("gy", 0), ("gz", 0))


def matchings():
    plan = []
    for axis in AXES:
        size = lax.axis_size(axis)
        for first in (0, 1):
            links = [(i, i + 1) for i in range(first, size - 1, 2)]
            if not links:
                continue
            if first == 1 and size % 2 == 0:
                links.append((size - 1, 0))
            plan.append((axis, [q for i, j in links for q in ((i, j), (j, i))], first))
    plan.sort(key=lambda entry: ORDER.index((entry[0], entry[2])))
    return plan


def bearings(plan):
    upward, block = [], [jnp.int32(-1)] * 6
    for number, (axis, _, first) in enumerate(plan):
        a, place, size = AXES.index(axis), lax.axis_index(axis), lax.axis_size(axis)
        rises = lax.rem(place, 2) == first
        upward.append((a, rises))
        for side in (0, 1):
            inside = (place > 0) if side == 0 else (place < size - 1)
            used = jnp.logical_and(rises if side == 1 else jnp.logical_not(rises), inside)
            block[2 * a + side] = jnp.where(used, number, block[2 * a + side])
    return upward, block


def coefficients(lower, upper):
    return [(upper ** (k + 1) - lower ** (k + 1)) / math.factorial(k + 1) for k in range(TERMS)]


def halves(x):
    hi = x.astype(BF)
    return hi, (x - hi.astype(F32)).astype(BF)


def dot(a, b):
    return jnp.dot(a, b, preferred_element_type=F32)


class Sizes:
    def __init__(self, fields, modes, faces, bases, members, width, messages):
        self.F, self.M, self.C, self.B, self.E = fields, modes, faces, bases, members
        self.W, self.K = width, messages
        self.H = members // 2
        self.FP = up(fields, 2) // 2
        self.MP = up(modes, 64)
        self.BP = up(bases, 8)
        self.BQ = up(bases, 16)
        self.R = fields * self.BP
        self.RP = up(self.R, 16)
        self.Q = members // width
        self.QR = up(up(self.R, 8 * self.Q) // self.Q, 8)
        self.KW = up(messages * width, 128)
        self.S = faces * members


def filled(x, rows):
    if x.shape[0] == rows:
        return x
    return jnp.concatenate([x, jnp.zeros((rows - x.shape[0], x.shape[1]), x.dtype)], axis=0)


def put_field(z, y3, f, x):
    hi, lo = halves(filled(x, z.MP))
    lanes = slice(f * z.E, (f + 1) * z.E)
    y3[0:z.MP, lanes] = hi
    y3[z.MP:2 * z.MP, lanes] = lo
    y3[2 * z.MP:3 * z.MP, lanes] = hi


def put_face(z, u, c, lanes, hi, lo):
    for part, value in enumerate((hi, lo, hi)):
        at = (part * z.C + c) * z.BQ
        u[at:at + z.BQ, lanes] = value


def lift(z, pt, u):
    return dot(pt[...], u[...])


def lane(z, i):
    return slice(i * z.E, (i + 1) * z.E)


def take(x, row):
    return jnp.take_along_axis(x, jnp.broadcast_to(row, x.shape), axis=1)


def low_lanes(z, rows):
    return lax.broadcasted_iota(jnp.int32, (rows, z.E), 1) < z.H


def balanced(z, out, matrix, y3):
    rows, lanes = matrix.shape[0], out.shape[1]
    even = lanes // (2 * z.E) * 2 * z.E
    out[0:rows, 0:even] = dot(matrix[...], y3[:, 0:even])
    if even < lanes:
        cut = up(rows // 2, 16)
        out[0:cut, even:lanes] = dot(matrix[0:cut, :], y3[:, even:lanes])
        out[cut:rows, even:lanes] = dot(matrix[cut:rows, :], y3[:, even:lanes])


def fold(z, first, second):
    low = low_lanes(z, first.shape[0])
    second = jnp.zeros_like(first) if second is None else second
    return jnp.where(low, first, second) + pltpu.roll(jnp.where(low, second, first), z.H, 1)


def compact(z, pick, field):
    low = low_lanes(z, z.M)
    out = []
    for p in range(z.FP):
        a = take(field(2 * p), pick)
        b = take(field(2 * p + 1), pick) if 2 * p + 1 < z.F else jnp.zeros_like(a)
        out.append(jnp.where(low, a, b))
    return out


def expand(z, rank, pairs, f):
    return take(pairs(f // 2), rank + z.H * (f % 2))


def star_sum(z, start, group, turned, star, count):
    total = list(start)
    for f in range(count):
        for d in range(3):
            t = turned[d * z.M:(d + 1) * z.M, lane(z, f)]
            for i, g in enumerate(group):
                term = star[g, f, d:d + 1, :] * t
                total[i] = term if total[i] is None else total[i] + term
    return total


def mark(ref, at, parts):
    for i, x in enumerate(parts):
        ref[pl.ds(pl.multiple_of(at, 8), 8), i * x.shape[1]:(i + 1) * x.shape[1]] = x[0:8, :]


def star_pair(z, p, turned, star):
    group = [g for g in (2 * p, 2 * p + 1) if g < z.F]
    total = star_sum(z, [None] * len(group), group, turned, star, z.FP)
    return fold(z, total[0], total[1] if len(group) == 2 else None)


def face_sum(z, flux, g, c, t):
    total = flux[g, 0, c:c + 1, :] * t[0]
    for f in range(1, len(t)):
        total = total + flux[g, f, c:c + 1, :] * t[f]
    return total


def face_rows(z, traces, c, count):
    return [traces[c * z.BP:(c + 1) * z.BP, lane(z, f)] for f in range(count)]


def groups_of(n, size):
    return [list(range(i, min(n, i + size))) for i in range(0, n, size)]


def regroup(z, base, part):
    group = lax.broadcasted_iota(jnp.int32, (z.QR, z.E), 1)
    out = None
    for q in range(z.Q):
        shift = (q - base) % z.Q * z.W
        x = part(q)
        x = pltpu.roll(x, shift, 1) if shift else x
        out = x if out is None else jnp.where(group >= q * z.W, x, out)
    return out


def ungroup(z, messages, q):
    group = lax.broadcasted_iota(jnp.int32, (z.QR, z.E), 1)
    out = None
    for m, message in enumerate(messages):
        shift = (m - q) % z.Q * z.W
        x = message[...]
        x = pltpu.roll(x, shift, 1) if shift else x
        out = x if out is None else jnp.where(group >= m * z.W, x, out)
    if len(messages) < z.Q:
        out = jnp.where(group < len(messages) * z.W, out, 0.0)
    return out


def pack_messages(z, sent, ohs, sx, messages, picked):
    hi, lo = halves(sent[...])
    sx[0:z.R, :] = hi
    sx[z.RP:z.RP + z.R, :] = lo
    both = dot(sx[...], ohs[...])
    picked[...] = both[0:z.R, :] + both[z.RP:z.RP + z.R, :]
    for m, message in enumerate(messages):
        home = lane(z, m // z.Q)
        message[...] = regroup(z, m % z.Q, lambda q: filled(picked[q * z.QR:min(z.R, (q + 1) * z.QR), home], z.QR))


def triple(rows, cols, target, wide, matrix):
    hi = matrix.astype(BF).astype(F32)
    wide[rows, 0:cols] = hi
    wide[rows, cols:2 * cols] = hi
    wide[rows, 2 * cols:3 * cols] = matrix - hi
    target[rows, :] = wide[rows, 0:3 * cols].astype(BF)


def first_kernel(z, plan, *refs):
    n = 10
    hbm, refs = refs[:n], refs[n:]
    (y, star, local, across, deriv, volume, partner, cluster, p3, square, ohs, y3, traces, sx), refs = refs[:14], refs[14:]
    messages, refs = refs[:z.K], refs[z.K:]
    projection, slots, sent, picked, picks, wide, sem = refs
    targets = (y, projection, slots, across, star, local, deriv, volume, partner, cluster)
    copies = [pltpu.make_async_copy(a, b, sem.at[i]) for i, (a, b) in enumerate(zip(hbm, targets))]
    for i in (2, 1, 0, 3, *range(4, n)):
        copies[i].start()
    square[...] = jnp.zeros_like(square)
    wide[...] = jnp.zeros_like(wide)
    picks[...] = jnp.full_like(picks, -1)
    upward, _ = bearings(plan)
    copies[2].wait()
    for m, (a, rises) in enumerate(upward):
        picks[0:1, m * z.W:(m + 1) * z.W] = jnp.where(rises, slots[2 * a + 1:2 * a + 2, :], slots[2 * a:2 * a + 1, :])
    ids = lax.broadcasted_iota(jnp.int32, (z.S, z.KW), 0)
    ohs[...] = jnp.where(ids == picks[0:1, :], 1.0, 0.0).astype(BF)
    copies[1].wait()
    for c in range(z.C):
        for b in range(z.B):
            square[c * z.BQ + b:c * z.BQ + b + 1, 0:z.M] = projection[b, c:c + 1, :]
    for c in range(z.C):
        rows = slice(c * z.BP, (c + 1) * z.BP)
        triple(rows, z.MP, p3, wide, square[c * z.BQ:c * z.BQ + z.BP, 0:z.MP])
    copies[0].wait()
    for f in range(z.F):
        put_field(z, y3, f, y[f * z.M:(f + 1) * z.M, :])
    traces[...] = dot(p3[...], y3[...])
    copies[3].wait()
    for c in range(z.C):
        t = face_rows(z, traces, c, z.F)
        for g in range(z.F):
            sent[g * z.BP:(g + 1) * z.BP, lane(z, c)] = face_sum(z, across, g, c, t)
    pack_messages(z, sent, ohs, sx, messages, picked)
    for copy in copies[4:]:
        copy.wait()


def set_up(z, plan, deriv, volume, square, partner, cluster, ohs, star, across, local, outs, scratch):
    s3, v3, pt, ohr, ohl, ohr_pairs, ohs_half, ohl_half, index, star_pairs, across_pairs, local_pairs = outs
    wide, block, picks = scratch
    wide[...] = jnp.zeros_like(wide)
    block[...] = jnp.zeros_like(block)
    for source, target in ((deriv, s3), (volume, v3)):
        for d in range(3):
            block[0:z.M, 0:z.M] = source[d]
            turned = jnp.transpose(block[...])
            triple(slice(d * z.M, (d + 1) * z.M), z.MP, target, wide, turned[0:z.M, 0:z.MP])
    triple(slice(0, z.M), z.C * z.BQ, pt, wide, jnp.transpose(square[...])[0:z.M, 0:z.C * z.BQ])
    _, arrival = bearings(plan)
    far = partner[...] - z.S
    moved = jnp.full_like(far, -1)
    for i in range(6):
        here = jnp.logical_and(far >= i * z.W, far < (i + 1) * z.W)
        here = jnp.logical_and(here, arrival[i] >= 0)
        moved = jnp.where(here, arrival[i] * z.W + far - i * z.W, moved)
    slots = partner[...]
    for c in range(z.C):
        ids = lax.broadcasted_iota(jnp.int32, (z.S, z.E), 0)
        ohl[:, lane(z, c)] = jnp.where(ids == slots[c:c + 1, :], 1.0, 0.0).astype(BF)
        ids = lax.broadcasted_iota(jnp.int32, (z.KW, z.E), 0)
        ohr[:, lane(z, c)] = jnp.where(ids == moved[c:c + 1, :], 1.0, 0.0).astype(BF)
    fast = cluster[...] == 0
    flags = jnp.broadcast_to(jnp.where(fast, 1.0, 0.0), (8, z.E))
    a = lax.broadcasted_iota(jnp.int32, (z.E, z.E), 0)
    b = lax.broadcasted_iota(jnp.int32, (z.E, z.E), 1)
    below = jnp.where(a <= b, 1.0, 0.0).astype(BF)
    running = dot(flags.astype(BF), below)
    count = dot(flags.astype(BF), jnp.ones((z.E, z.E), BF))
    rank = running[0:1, :].astype(jnp.int32) - 1
    held = jnp.where(fast, rank, -1)
    chosen = jnp.where(lax.broadcasted_iota(jnp.int32, (z.H, z.E), 0) == held, 1.0, 0.0).astype(BF)
    numbers = lax.broadcasted_iota(jnp.int32, (8, z.E), 1).astype(F32).astype(BF)
    listed = lax.dot_general(numbers, chosen, (((1,), (1,)), ((), ())), preferred_element_type=F32)
    picks[:, 0:z.H] = listed
    picks[:, z.H:2 * z.H] = listed
    pick = picks[0:1, :].astype(jnp.int32)
    place = lax.broadcasted_iota(jnp.int32, (1, z.E), 1)
    place = jnp.where(place < z.H, place, place - z.H)
    live = place < count[0:1, :].astype(jnp.int32)
    index[...] = jnp.zeros_like(index)
    index[0:1, :] = pick
    index[1:2, :] = jnp.maximum(rank, 0)
    index[2:3, :] = jnp.where(fast, 1, 0)
    both = jnp.concatenate([chosen, chosen], axis=0)
    for c in range(z.C):
        pairs = lax.dot_general(ohr[:, lane(z, c)], both, (((1,), (1,)), ((), ())), preferred_element_type=F32)
        ohr_pairs[:, lane(z, c)] = pairs.astype(BF)
        rows = slice(c * z.H, (c + 1) * z.H)
        ohs_half[rows, :] = dot(chosen, ohs[lane(z, c), :]).astype(BF)
        ohl_half[rows, :] = dot(chosen, ohl[lane(z, c), :]).astype(BF)
    for source, target in ((star, star_pairs), (across, across_pairs), (local, local_pairs)):
        low = jnp.logical_and(low_lanes(z, 1), live)
        high = jnp.logical_and(jnp.logical_not(low_lanes(z, 1)), live)
        for g in range(z.F):
            for p in range(z.FP):
                value = jnp.where(low, take(source[g, 2 * p], pick), 0.0)
                if 2 * p + 1 < z.F:
                    value = jnp.where(high, take(source[g, 2 * p + 1], pick), value)
                target[g, p] = value


def first_local_kernel(z, plan, *refs):
    deriv, volume, square, partner, cluster, ohs, star, across, local, y3, traces, sx = refs[:12]
    outs, src, half, refs = refs[12:24], refs[24], refs[25], refs[26:]
    turned, u, gathered, *scratch = refs
    set_up(z, plan, deriv, volume, square, partner, cluster, ohs, star, across, local, outs, scratch)
    v3, pt, ohl = outs[1], outs[2], outs[4]
    turned[...] = dot(v3[...], y3[...])
    gathered[...] = dot(sx[...], ohl[...])
    for c in range(z.C):
        t = face_rows(z, traces, c, z.F)
        for g in range(z.F):
            total = gathered[g * z.BP:(g + 1) * z.BP, lane(z, c)] + gathered[z.RP + g * z.BP:z.RP + (g + 1) * z.BP, lane(z, c)]
            hi, lo = halves(filled(total + face_sum(z, local, g, c, t), z.BQ))
            put_face(z, u, c, lane(z, g), hi, lo)
    lifted = lift(z, pt, u)
    for group in groups_of(z.F, 3):
        start = [lifted[:, lane(z, g)] for g in group]
        for g, total in zip(group, star_sum(z, start, group, turned, star, z.F)):
            src[g * z.M:(g + 1) * z.M, :] = total
    index = outs[8]
    for p, value in enumerate(compact(z, index[0:1, :], lambda f: src[f * z.M:(f + 1) * z.M, :])):
        half[p * z.M:(p + 1) * z.M, :] = value


def lift_gathered(z, gathered, u, pt):
    for c in range(z.C):
        for g in range(z.F):
            hi = filled(gathered[g * z.BP:(g + 1) * z.BP, lane(z, c)], z.BQ).astype(BF)
            lo = filled(gathered[z.RP + g * z.BP:z.RP + (g + 1) * z.BP, lane(z, c)], z.BQ).astype(BF)
            put_face(z, u, c, lane(z, g), hi, lo)
    return lift(z, pt, u)


def local_kernel(z, last, *refs):
    y3, traces, sx, v3, pt, star, local, ohl, index, src_in, half_in, stacked, ohr = refs[:13]
    refs = refs[13:]
    if last:
        older, start, moved, refs = refs[0:2], refs[2], refs[3], refs[4:]
        src_out, weights, base, half_out, refs = refs[0], refs[1], refs[2], refs[3], refs[4:]
    else:
        src_full, src_out, half_out, refs = refs[0], refs[1], refs[2], refs[3:]
    turned, u, gathered, u_half, lifted, u_far, gathered_far, landed = refs
    gathered_far[...] = dot(stacked[...], ohr[...])
    landed[...] = lift_gathered(z, gathered_far, u_far, pt)
    turned[...] = dot(v3[...], y3[...])
    gathered[...] = dot(sx[...], ohl[...])
    for c in range(z.C):
        t = face_rows(z, traces, c, z.FP)
        for p in range(z.FP):
            first = face_sum(z, local, 2 * p, c, t)
            second = face_sum(z, local, 2 * p + 1, c, t) if 2 * p + 1 < z.F else None
            hi, lo = halves(filled(fold(z, first, second), z.BQ))
            put_face(z, u_half, c, lane(z, p), hi, lo)
    lifted_half = lift(z, pt, u_half)
    lifted[...] = lift_gathered(z, gathered, u, pt)
    pick, rank = index[0:1, :], index[1:2, :]
    gained = compact(z, pick, lambda f: lifted[:, lane(z, f)])
    for p in range(z.FP):
        rows = slice(p * z.M, (p + 1) * z.M)
        half_out[rows, :] = half_in[rows, :] + gained[p] + lifted_half[:, lane(z, p)] + star_pair(z, p, turned, star)
    fast = index[2:3, :] > 0
    for g in range(z.F):
        rows = slice(g * z.M, (g + 1) * z.M)
        whole = src_in[rows, :] + landed[:, lane(z, g)]
        value = whole + lifted[:, lane(z, g)]
        if last:
            pairs = lambda p: half_out[p * z.M:(p + 1) * z.M, :]
            src_out[rows, :] = jnp.where(fast, expand(z, rank, pairs, g), value)
            pairs = lambda p: moved[p * z.M:(p + 1) * z.M, :]
            base[rows, :] = start[rows, :] + jnp.where(fast, expand(z, rank, pairs, g), 0.0)
            sources = [x[rows, :] for x in older] + [whole]
            sources = [jnp.where(fast, 0.0, x) for x in sources]
            for k in range(TERMS):
                total = None
                for step, x in zip(range(FINE_STEPS - 1, 0, -1), sources):
                    c = coefficients(step / FINE_STEPS, (step + 1) / FINE_STEPS)[k]
                    total = c * x if total is None else total + c * x
                weights[k, rows, :] = total
        else:
            src_full[rows, :] = whole
            src_out[rows, :] = value


def arrive(z, arrived, landed, stacked):
    for i, group in enumerate(groups_of(z.K, z.Q)):
        for q in range(z.Q):
            rows = min(z.R, (q + 1) * z.QR) - q * z.QR
            landed[q * z.QR:q * z.QR + rows, lane(z, i)] = ungroup(z, [arrived[m] for m in group], q)[0:rows, :]
    hi, lo = halves(landed[...])
    stacked[0:z.R, :] = hi
    stacked[z.RP:z.RP + z.R, :] = lo


def lift_pairs(z, gathered, u, pt):
    low = low_lanes(z, z.BP)
    for c in range(z.C):
        for p in range(z.FP):
            parts = []
            for at in (0, z.RP):
                a = gathered[at + 2 * p * z.BP:at + (2 * p + 1) * z.BP, lane(z, c)]
                b = gathered[at + (2 * p + 1) * z.BP:at + (2 * p + 2) * z.BP, lane(z, c)] if 2 * p + 1 < z.F else 0.0
                parts.append(filled(jnp.where(low, a, b), z.BQ).astype(BF))
            put_face(z, u, c, lane(z, p), *parts)
    return lift(z, pt, u)


def step_kernel(z, first, *refs):
    arrived, refs = refs[:z.K], refs[z.K:]
    half_in, moved_in, s3, p3, pt, star, across, ohr, ohs = refs[:9]
    half, moved, y3, traces, sx, stacked = refs[9:15]
    messages, refs = refs[15:15 + z.K], refs[15 + z.K:]
    landed, gathered, u, turned, other, change, sent, picked = refs
    arrive(z, arrived, landed, stacked)
    gathered[...] = dot(stacked[...], ohr[...])
    gained = lift_pairs(z, gathered, u, pt)
    row = coefficients(0.0, 1.0 / FINE_STEPS)
    for p in range(z.FP):
        rows = slice(p * z.M, (p + 1) * z.M)
        value = half_in[rows, :] + gained[:, lane(z, p)]
        half[rows, :] = value
        put_field(z, y3, p, row[TERMS - 1] * value)

    buffers = (turned, other)

    def product(out, pairs):
        lanes = slice(pairs[0] * z.E, (pairs[-1] + 1) * z.E)
        out[:, lanes] = dot(s3[...], y3[:, lanes])

    tiles = groups_of(z.FP, 2)
    for pairs in tiles:
        product(turned, pairs)
    for k in range(TERMS - 2, -1, -1):
        now, later = buffers if k % 2 == 0 else buffers[::-1]
        for pairs in tiles:
            for p in pairs:
                rows = slice(p * z.M, (p + 1) * z.M)
                total = row[k] * half[rows, :] + star_pair(z, p, now, star)
                if k > 0:
                    put_field(z, y3, p, total)
                else:
                    change[rows, :] = total
            if k > 0:
                product(later, pairs)
    moved[...] = change[...] if first else moved_in[...] + change[...]
    for p in range(z.FP):
        put_field(z, y3, p, change[p * z.M:(p + 1) * z.M, :])
    traces[...] = dot(p3[...], y3[...])
    for pair in groups_of(z.C, 2):
        t = [face_rows(z, traces, c, z.FP) for c in pair]
        for g in range(z.F):
            total = fold(z, *[face_sum(z, across, g, c, t[i]) for i, c in enumerate(pair)])
            sent[g * z.BP:(g + 1) * z.BP, lane(z, pair[0] // 2)] = total
    pack_messages(z, sent, ohs, sx, messages, picked)


def last_kernel(z, *refs):
    arrived, refs = refs[:z.K], refs[z.K:]
    src_in, weights, base, s3, pt, star, ohr, out = refs[:8]
    landed, stacked, gathered, u, lifted, turned, y3, src = refs[8:]
    arrive(z, arrived, landed, stacked)
    gathered[...] = dot(stacked[...], ohr[...])
    lifted[...] = lift_gathered(z, gathered, u, pt)
    row = coefficients(0.0, 1.0 / FINE_STEPS)
    for g in range(z.F):
        rows = slice(g * z.M, (g + 1) * z.M)
        value = src_in[rows, :] + lifted[:, lane(z, g)]
        src[rows, :] = value
        put_field(z, y3, g, weights[TERMS - 1, rows, :] + row[TERMS - 1] * value)

    def term(i, carry):
        c = F32(row[TERMS - 2])
        for k in range(TERMS - 2):
            c = jnp.where(i == TERMS - 2 - k, F32(row[k]), c)
        turned[0:3 * z.M, :] = dot(s3[...], y3[...])
        for group in groups_of(z.F, 2):
            start = [weights[TERMS - 2 - i, g * z.M:(g + 1) * z.M, :] + c * src[g * z.M:(g + 1) * z.M, :] for g in group]
            sums = star_sum(z, start, group, turned, star, z.F)
            mark(turned, 3 * z.M + 8 * i, sums)
            for g, total in zip(group, sums):
                put_field(z, y3, g, total)
                out[g * z.M:(g + 1) * z.M, :] = total
        return carry

    lax.fori_loop(0, TERMS - 1, term, 0)
    out[...] = out[...] + base[...]


def call(kernel, outs, scratch, *args, remote=False):
    place = pl.BlockSpec(memory_space=pltpu.HBM if remote else pltpu.VMEM)
    if remote:
        args = [pltpu.with_memory_space_constraint(x, pltpu.HBM) for x in args]
    vmem = pl.BlockSpec(memory_space=pltpu.VMEM)
    return pl.pallas_call(
        kernel,
        out_shape=[jax.ShapeDtypeStruct(*o) for o in outs],
        in_specs=[place] * len(args),
        out_specs=[vmem] * len(outs),
        scratch_shapes=[pltpu.VMEM(*o) if isinstance(o, tuple) else o for o in scratch],
        compiler_params=pltpu.CompilerParams(vmem_limit_bytes=24 << 20),
        cost_estimate=pl.CostEstimate(flops=1 << 30, bytes_accessed=2 << 20, transcendentals=0),
    )(*args)


def body(
    final_adjoint,
    star_mats,
    deriv_stiff,
    volume_stiffness,
    face_projection,
    flux_local,
    flux_across,
    cluster,
    partner,
    send_slots,
):
    fields, modes, members = final_adjoint.shape
    faces, bases, _ = face_projection.shape
    plan = matchings()
    width = send_slots.shape[1]
    z = Sizes(fields, modes, faces, bases, members, width, len(plan))

    full, half = ((fields * modes, members), F32), ((z.FP * modes, members), F32)
    y3, y3_half = ((3 * z.MP, fields * members), BF), ((3 * z.MP, z.FP * members), BF)
    traces, traces_half = ((faces * z.BP, fields * members), F32), ((faces * z.BP, z.FP * members), F32)
    turned, turned_half = ((3 * modes, fields * members), F32), ((3 * modes, z.FP * members), F32)
    marked = lambda o: ((o[0][0] + 8 * (TERMS - 1), o[0][1]), o[1])
    u, u_half = ((3 * faces * z.BQ, fields * members), BF), ((3 * faces * z.BQ, z.FP * members), BF)
    gathered, lifted = ((2 * z.RP, z.S), F32), ((modes, fields * members), F32)
    landed, stacked = ((z.R, z.KW), F32), ((2 * z.RP, z.KW), BF)
    sx, sx_half = ((2 * z.RP, z.S), BF), ((2 * z.RP, z.S // 2), BF)
    sent, sent_half, picked = ((z.R, z.S), F32), ((z.R, z.S // 2), F32), ((z.R, z.KW), F32)
    messages_out = [((z.QR, members), F32)] * z.K
    wide = ((3 * modes, up(3 * max(z.MP, faces * z.BQ), 128)), F32)
    pairs = lambda n: ((fields, z.FP, n, members), F32)

    def trade(messages):
        return [lax.ppermute(m, axis, links) for m, (axis, links, _) in zip(messages, plan)]

    star = jnp.transpose(star_mats, (1, 2, 0, 3))
    local = jnp.transpose(flux_local, (1, 2, 0, 3))
    across = jnp.transpose(flux_across, (1, 2, 0, 3))
    args = [
        final_adjoint.reshape(fields * modes, members), jnp.transpose(face_projection, (1, 0, 2)), send_slots, across,
        star, local, deriv_stiff, volume_stiffness, partner, cluster.reshape(1, members),
    ]
    like = lambda x: (x.shape, x.dtype)
    (start, star, local, across, deriv, volume, partner, cluster, p3, square, ohs, y3v, tr, sxv, *messages) = call(
        functools.partial(first_kernel, z, plan),
        [like(args[i]) for i in (0, 4, 5, 3, 6, 7, 8, 9)]
        + [((faces * z.BP, 3 * z.MP), BF), ((128, 128), F32), ((z.S, z.KW), BF), y3, traces, sx] + messages_out,
        [like(args[1]), like(args[2]), sent, picked, ((8, z.KW), jnp.int32), wide, pltpu.SemaphoreType.DMA((len(args),))],
        *args, remote=True,
    )
    arrived = trade(messages)
    s3, v3, pt, ohr, ohl, ohr_pairs, ohs_half, ohl_half, index, star_pairs, across_pairs, local_pairs, src, half_src = call(
        functools.partial(first_local_kernel, z, plan),
        [((3 * modes, 3 * z.MP), BF), ((3 * modes, 3 * z.MP), BF), ((modes, 3 * faces * z.BQ), BF), ((z.KW, z.S), BF),
         ((z.S, z.S), BF), ((z.KW, z.S), BF), ((z.S // 2, z.KW), BF), ((z.S // 2, z.S), BF), ((8, members), jnp.int32),
         pairs(3), pairs(faces), pairs(faces), full, half],
        [turned, u, gathered, wide, ((128, 128), F32), ((8, members), F32)],
        deriv, volume, square, partner, cluster, ohs, star, across, local, y3v, tr, sxv,
    )
    moved = jnp.zeros((8, members), F32)
    sources = []
    for step in range(FINE_STEPS - 1, 0, -1):
        half_src, moved, y3v, tr, sxv, stack, *messages = call(
            functools.partial(step_kernel, z, step == FINE_STEPS - 1),
            [half, half, y3_half, traces_half, sx_half, stacked] + messages_out,
            [landed, gathered, u_half, turned_half, turned_half, half, sent_half, picked],
            *arrived, half_src, moved, s3, p3, pt, star_pairs, across_pairs, ohr_pairs, ohs_half,
        )
        arrived = trade(messages)
        last = step == 1
        local_args = [y3v, tr, sxv, v3, pt, star_pairs, local_pairs, ohl_half, index, src, half_src, stack, ohr]
        local_scratch = [turned_half, u, gathered, u_half, lifted, u, gathered, lifted]
        if last:
            src, weights, base, _ = call(
                functools.partial(local_kernel, z, True), [full, ((TERMS,) + full[0], F32), full, half], local_scratch,
                *local_args, *sources, start, moved,
            )
        else:
            whole, src, half_src = call(functools.partial(local_kernel, z, False), [full, full, half], local_scratch, *local_args)
            sources.append(whole)
    (out,) = call(
        functools.partial(last_kernel, z), [full],
        [landed, stacked, gathered, u, lifted, marked(turned), y3, full],
        *arrived, src, weights, base, s3, pt, star, ohr,
    )
    return out.reshape(fields, modes, members)


def solution(mesh):
    in_specs = (
        P(None, None, ("gx", "gy", "gz")),
        P(None, None, None, ("gx", "gy", "gz")),
        P(),
        P(),
        P(),
        P(None, None, None, ("gx", "gy", "gz")),
        P(None, None, None, ("gx", "gy", "gz")),
        P(("gx", "gy", "gz")),
        P(None, ("gx", "gy", "gz")),
        P(None, ("gx", "gy", "gz")),
    )
    out_specs = P(None, None, ("gx", "gy", "gz"))
    return jax.shard_map(body, mesh=mesh, in_specs=in_specs, out_specs=out_specs, check_vma=False)
```

```python
import functools
import math

import jax
import jax.numpy as jnp
from jax import lax
from jax.experimental import pallas as pl
from jax.experimental.pallas import tpu as pltpu
from jax.sharding import PartitionSpec as P

TERMS = 6
FINE_STEPS = 4
BF = jnp.bfloat16
F32 = jnp.float32


def up(n, unit):
    return -(-n // unit) * unit


AXES = ("gx", "gy", "gz")
ORDER = (("gx", 1), ("gz", 1), ("gx", 0), ("gy", 1), ("gy", 0), ("gz", 0))


def matchings():
    plan = []
    for axis in AXES:
        size = lax.axis_size(axis)
        for first in (0, 1):
            links = [(i, i + 1) for i in range(first, size - 1, 2)]
            if not links:
                continue
            if first == 1 and size % 2 == 0:
                links.append((size - 1, 0))
            plan.append((axis, [q for i, j in links for q in ((i, j), (j, i))], first))
    plan.sort(key=lambda entry: ORDER.index((entry[0], entry[2])))
    return plan


def bearings(plan):
    upward, block = [], [jnp.int32(-1)] * 6
    for number, (axis, _, first) in enumerate(plan):
        a, place, size = AXES.index(axis), lax.axis_index(axis), lax.axis_size(axis)
        rises = lax.rem(place, 2) == first
        upward.append((a, rises))
        for side in (0, 1):
            inside = (place > 0) if side == 0 else (place < size - 1)
            used = jnp.logical_and(rises if side == 1 else jnp.logical_not(rises), inside)
            block[2 * a + side] = jnp.where(used, number, block[2 * a + side])
    return upward, block


def coefficients(lower, upper):
    return [(upper ** (k + 1) - lower ** (k + 1)) / math.factorial(k + 1) for k in range(TERMS)]


def halves(x):
    hi = x.astype(BF)
    return hi, (x - hi.astype(F32)).astype(BF)


def dot(a, b):
    return jnp.dot(a, b, preferred_element_type=F32)


class Sizes:
    def __init__(self, fields, modes, faces, bases, members, width, messages):
        self.F, self.M, self.C, self.B, self.E = fields, modes, faces, bases, members
        self.W, self.K = width, messages
        self.H = members // 2
        self.FP = up(fields, 2) // 2
        self.MP = up(modes, 64)
        self.BP = up(bases, 8)
        self.BQ = up(bases, 16)
        self.R = fields * self.BP
        self.RP = up(self.R, 16)
        self.Q = members // width
        self.QR = up(up(self.R, 8 * self.Q) // self.Q, 8)
        self.KW = up(messages * width, 128)
        self.S = faces * members


def filled(x, rows):
    if x.shape[0] == rows:
        return x
    return jnp.concatenate([x, jnp.zeros((rows - x.shape[0], x.shape[1]), x.dtype)], axis=0)


def put_field(z, y3, f, x):
    hi, lo = halves(filled(x, z.MP))
    lanes = slice(f * z.E, (f + 1) * z.E)
    y3[0:z.MP, lanes] = hi
    y3[z.MP:2 * z.MP, lanes] = lo
    y3[2 * z.MP:3 * z.MP, lanes] = hi


def put_face(z, u, c, lanes, hi, lo):
    for part, value in enumerate((hi, lo, hi)):
        at = (part * z.C + c) * z.BQ
        u[at:at + z.BQ, lanes] = value


def lift(z, pt, u):
    return dot(pt[...], u[...])


def lane(z, i):
    return slice(i * z.E, (i + 1) * z.E)


def take(x, row):
    return jnp.take_along_axis(x, jnp.broadcast_to(row, x.shape), axis=1)


def low_lanes(z, rows):
    return lax.broadcasted_iota(jnp.int32, (rows, z.E), 1) < z.H


def balanced(z, out, matrix, y3):
    rows, lanes = matrix.shape[0], out.shape[1]
    even = lanes // (2 * z.E) * 2 * z.E
    out[0:rows, 0:even] = dot(matrix[...], y3[:, 0:even])
    if even < lanes:
        cut = up(rows // 2, 16)
        out[0:cut, even:lanes] = dot(matrix[0:cut, :], y3[:, even:lanes])
        out[cut:rows, even:lanes] = dot(matrix[cut:rows, :], y3[:, even:lanes])


def fold(z, first, second):
    low = low_lanes(z, first.shape[0])
    second = jnp.zeros_like(first) if second is None else second
    return jnp.where(low, first, second) + pltpu.roll(jnp.where(low, second, first), z.H, 1)


def compact(z, pick, field):
    low = low_lanes(z, z.M)
    out = []
    for p in range(z.FP):
        a = take(field(2 * p), pick)
        b = take(field(2 * p + 1), pick) if 2 * p + 1 < z.F else jnp.zeros_like(a)
        out.append(jnp.where(low, a, b))
    return out


def expand(z, rank, pairs, f):
    return take(pairs(f // 2), rank + z.H * (f % 2))


def star_sum(z, start, group, turned, star, count):
    total = list(start)
    for f in range(count):
        for d in range(3):
            t = turned[d * z.M:(d + 1) * z.M, lane(z, f)]
            for i, g in enumerate(group):
                term = star[g, f, d:d + 1, :] * t
                total[i] = term if total[i] is None else total[i] + term
    return total


def mark(ref, at, parts):
    for i, x in enumerate(parts):
        ref[pl.ds(pl.multiple_of(at, 8), 8), i * x.shape[1]:(i + 1) * x.shape[1]] = x[0:8, :]


def star_pair(z, p, turned, star):
    group = [g for g in (2 * p, 2 * p + 1) if g < z.F]
    total = star_sum(z, [None] * len(group), group, turned, star, z.FP)
    return fold(z, total[0], total[1] if len(group) == 2 else None)


def face_sum(z, flux, g, c, t):
    total = flux[g, 0, c:c + 1, :] * t[0]
    for f in range(1, len(t)):
        total = total + flux[g, f, c:c + 1, :] * t[f]
    return total


def face_rows(z, traces, c, count):
    return [traces[c * z.BP:(c + 1) * z.BP, lane(z, f)] for f in range(count)]


def groups_of(n, size):
    return [list(range(i, min(n, i + size))) for i in range(0, n, size)]


def regroup(z, base, part):
    group = lax.broadcasted_iota(jnp.int32, (z.QR, z.E), 1)
    out = None
    for q in range(z.Q):
        shift = (q - base) % z.Q * z.W
        x = part(q)
        x = pltpu.roll(x, shift, 1) if shift else x
        out = x if out is None else jnp.where(group >= q * z.W, x, out)
    return out


def ungroup(z, messages, q):
    group = lax.broadcasted_iota(jnp.int32, (z.QR, z.E), 1)
    out = None
    for m, message in enumerate(messages):
        shift = (m - q) % z.Q * z.W
        x = message[...]
        x = pltpu.roll(x, shift, 1) if shift else x
        out = x if out is None else jnp.where(group >= m * z.W, x, out)
    if len(messages) < z.Q:
        out = jnp.where(group < len(messages) * z.W, out, 0.0)
    return out


def pack_messages(z, sent, ohs, sx, messages, picked):
    hi, lo = halves(sent[...])
    sx[0:z.R, :] = hi
    sx[z.RP:z.RP + z.R, :] = lo
    both = dot(sx[...], ohs[...])
    picked[...] = both[0:z.R, :] + both[z.RP:z.RP + z.R, :]
    for m, message in enumerate(messages):
        home = lane(z, m // z.Q)
        message[...] = regroup(z, m % z.Q, lambda q: filled(picked[q * z.QR:min(z.R, (q + 1) * z.QR), home], z.QR))


def triple(rows, cols, target, wide, matrix):
    hi = matrix.astype(BF).astype(F32)
    wide[rows, 0:cols] = hi
    wide[rows, cols:2 * cols] = hi
    wide[rows, 2 * cols:3 * cols] = matrix - hi
    target[rows, :] = wide[rows, 0:3 * cols].astype(BF)


def first_kernel(z, plan, *refs):
    n = 10
    hbm, refs = refs[:n], refs[n:]
    (y, star, local, across, deriv, volume, partner, cluster, p3, square, ohs, y3, traces, sx), refs = refs[:14], refs[14:]
    messages, refs = refs[:z.K], refs[z.K:]
    projection, slots, sent, picked, picks, wide, sem = refs
    targets = (y, projection, slots, across, star, local, deriv, volume, partner, cluster)
    copies = [pltpu.make_async_copy(a, b, sem.at[i]) for i, (a, b) in enumerate(zip(hbm, targets))]
    for i in (2, 1, 0, 3, *range(4, n)):
        copies[i].start()
    square[...] = jnp.zeros_like(square)
    wide[...] = jnp.zeros_like(wide)
    picks[...] = jnp.full_like(picks, -1)
    copies[1].wait()
    for c in range(z.C):
        for b in range(z.B):
            square[c * z.BQ + b:c * z.BQ + b + 1, 0:z.M] = projection[b, c:c + 1, :]
    for c in range(z.C):
        rows = slice(c * z.BP, (c + 1) * z.BP)
        triple(rows, z.MP, p3, wide, square[c * z.BQ:c * z.BQ + z.BP, 0:z.MP])
    copies[0].wait()
    for f in range(z.F):
        put_field(z, y3, f, y[f * z.M:(f + 1) * z.M, :])
    copies[3].wait()
    upward, _ = bearings(plan)
    copies[2].wait()
    for m, (a, rises) in enumerate(upward):
        picks[0:1, m * z.W:(m + 1) * z.W] = jnp.where(rises, slots[2 * a + 1:2 * a + 2, :], slots[2 * a:2 * a + 1, :])
    ids = lax.broadcasted_iota(jnp.int32, (z.S, z.KW), 0)
    ohs[...] = jnp.where(ids == picks[0:1, :], 1.0, 0.0).astype(BF)
    traces[...] = dot(p3[...], y3[...])
    for c in range(z.C):
        t = face_rows(z, traces, c, z.F)
        for g in range(z.F):
            sent[g * z.BP:(g + 1) * z.BP, lane(z, c)] = face_sum(z, across, g, c, t)
    pack_messages(z, sent, ohs, sx, messages, picked)
    for copy in copies[4:]:
        copy.wait()


def set_up(z, plan, deriv, volume, square, partner, cluster, ohs, star, across, local, outs, scratch):
    s3, v3, pt, ohr, ohl, ohr_pairs, ohs_half, ohl_half, index, star_pairs, across_pairs, local_pairs = outs
    wide, block, picks = scratch
    wide[...] = jnp.zeros_like(wide)
    block[...] = jnp.zeros_like(block)
    for source, target in ((deriv, s3), (volume, v3)):
        for d in range(3):
            block[0:z.M, 0:z.M] = source[d]
            turned = jnp.transpose(block[...])
            triple(slice(d * z.M, (d + 1) * z.M), z.MP, target, wide, turned[0:z.M, 0:z.MP])
    triple(slice(0, z.M), z.C * z.BQ, pt, wide, jnp.transpose(square[...])[0:z.M, 0:z.C * z.BQ])
    _, arrival = bearings(plan)
    far = partner[...] - z.S
    moved = jnp.full_like(far, -1)
    for i in range(6):
        here = jnp.logical_and(far >= i * z.W, far < (i + 1) * z.W)
        here = jnp.logical_and(here, arrival[i] >= 0)
        moved = jnp.where(here, arrival[i] * z.W + far - i * z.W, moved)
    slots = partner[...]
    for c in range(z.C):
        ids = lax.broadcasted_iota(jnp.int32, (z.S, z.E), 0)
        ohl[:, lane(z, c)] = jnp.where(ids == slots[c:c + 1, :], 1.0, 0.0).astype(BF)
        ids = lax.broadcasted_iota(jnp.int32, (z.KW, z.E), 0)
        ohr[:, lane(z, c)] = jnp.where(ids == moved[c:c + 1, :], 1.0, 0.0).astype(BF)
    fast = cluster[...] == 0
    flags = jnp.broadcast_to(jnp.where(fast, 1.0, 0.0), (8, z.E))
    a = lax.broadcasted_iota(jnp.int32, (z.E, z.E), 0)
    b = lax.broadcasted_iota(jnp.int32, (z.E, z.E), 1)
    below = jnp.where(a <= b, 1.0, 0.0).astype(BF)
    running = dot(flags.astype(BF), below)
    count = dot(flags.astype(BF), jnp.ones((z.E, z.E), BF))
    rank = running[0:1, :].astype(jnp.int32) - 1
    held = jnp.where(fast, rank, -1)
    chosen = jnp.where(lax.broadcasted_iota(jnp.int32, (z.H, z.E), 0) == held, 1.0, 0.0).astype(BF)
    numbers = lax.broadcasted_iota(jnp.int32, (8, z.E), 1).astype(F32).astype(BF)
    listed = lax.dot_general(numbers, chosen, (((1,), (1,)), ((), ())), preferred_element_type=F32)
    picks[:, 0:z.H] = listed
    picks[:, z.H:2 * z.H] = listed
    pick = picks[0:1, :].astype(jnp.int32)
    place = lax.broadcasted_iota(jnp.int32, (1, z.E), 1)
    place = jnp.where(place < z.H, place, place - z.H)
    live = place < count[0:1, :].astype(jnp.int32)
    index[...] = jnp.zeros_like(index)
    index[0:1, :] = pick
    index[1:2, :] = jnp.maximum(rank, 0)
    index[2:3, :] = jnp.where(fast, 1, 0)
    both = jnp.concatenate([chosen, chosen], axis=0)
    for c in range(z.C):
        pairs = lax.dot_general(ohr[:, lane(z, c)], both, (((1,), (1,)), ((), ())), preferred_element_type=F32)
        ohr_pairs[:, lane(z, c)] = pairs.astype(BF)
        rows = slice(c * z.H, (c + 1) * z.H)
        ohs_half[rows, :] = dot(chosen, ohs[lane(z, c), :]).astype(BF)
        ohl_half[rows, :] = dot(chosen, ohl[lane(z, c), :]).astype(BF)
    for source, target in ((star, star_pairs), (across, across_pairs), (local, local_pairs)):
        low = jnp.logical_and(low_lanes(z, 1), live)
        high = jnp.logical_and(jnp.logical_not(low_lanes(z, 1)), live)
        for g in range(z.F):
            for p in range(z.FP):
                value = jnp.where(low, take(source[g, 2 * p], pick), 0.0)
                if 2 * p + 1 < z.F:
                    value = jnp.where(high, take(source[g, 2 * p + 1], pick), value)
                target[g, p] = value


def first_local_kernel(z, plan, *refs):
    deriv, volume, square, partner, cluster, ohs, star, across, local, y3, traces, sx = refs[:12]
    outs, src, half, refs = refs[12:24], refs[24], refs[25], refs[26:]
    turned, u, gathered, *scratch = refs
    set_up(z, plan, deriv, volume, square, partner, cluster, ohs, star, across, local, outs, scratch)
    v3, pt, ohl = outs[1], outs[2], outs[4]
    turned[...] = dot(v3[...], y3[...])
    gathered[...] = dot(sx[...], ohl[...])
    for c in range(z.C):
        t = face_rows(z, traces, c, z.F)
        for g in range(z.F):
            total = gathered[g * z.BP:(g + 1) * z.BP, lane(z, c)] + gathered[z.RP + g * z.BP:z.RP + (g + 1) * z.BP, lane(z, c)]
            hi, lo = halves(filled(total + face_sum(z, local, g, c, t), z.BQ))
            put_face(z, u, c, lane(z, g), hi, lo)
    lifted = lift(z, pt, u)
    for group in groups_of(z.F, 3):
        start = [lifted[:, lane(z, g)] for g in group]
        for g, total in zip(group, star_sum(z, start, group, turned, star, z.F)):
            src[g * z.M:(g + 1) * z.M, :] = total
    index = outs[8]
    for p, value in enumerate(compact(z, index[0:1, :], lambda f: src[f * z.M:(f + 1) * z.M, :])):
        half[p * z.M:(p + 1) * z.M, :] = value


def lift_gathered(z, gathered, u, pt):
    for c in range(z.C):
        for g in range(z.F):
            hi = filled(gathered[g * z.BP:(g + 1) * z.BP, lane(z, c)], z.BQ).astype(BF)
            lo = filled(gathered[z.RP + g * z.BP:z.RP + (g + 1) * z.BP, lane(z, c)], z.BQ).astype(BF)
            put_face(z, u, c, lane(z, g), hi, lo)
    return lift(z, pt, u)


def local_kernel(z, last, *refs):
    y3, traces, sx, v3, pt, star, local, ohl, index, src_in, half_in, stacked, ohr = refs[:13]
    refs = refs[13:]
    if last:
        older, start, moved, refs = refs[0:2], refs[2], refs[3], refs[4:]
        src_out, weights, base, half_out, refs = refs[0], refs[1], refs[2], refs[3], refs[4:]
    else:
        src_full, src_out, half_out, refs = refs[0], refs[1], refs[2], refs[3:]
    turned, u, gathered, u_half, lifted, u_far, gathered_far, landed = refs
    gathered_far[...] = dot(stacked[...], ohr[...])
    landed[...] = lift_gathered(z, gathered_far, u_far, pt)
    turned[...] = dot(v3[...], y3[...])
    gathered[...] = dot(sx[...], ohl[...])
    for c in range(z.C):
        t = face_rows(z, traces, c, z.FP)
        for p in range(z.FP):
            first = face_sum(z, local, 2 * p, c, t)
            second = face_sum(z, local, 2 * p + 1, c, t) if 2 * p + 1 < z.F else None
            hi, lo = halves(filled(fold(z, first, second), z.BQ))
            put_face(z, u_half, c, lane(z, p), hi, lo)
    lifted_half = lift(z, pt, u_half)
    lifted[...] = lift_gathered(z, gathered, u, pt)
    pick, rank = index[0:1, :], index[1:2, :]
    gained = compact(z, pick, lambda f: lifted[:, lane(z, f)])
    for p in range(z.FP):
        rows = slice(p * z.M, (p + 1) * z.M)
        half_out[rows, :] = half_in[rows, :] + gained[p] + lifted_half[:, lane(z, p)] + star_pair(z, p, turned, star)
    fast = index[2:3, :] > 0
    for g in range(z.F):
        rows = slice(g * z.M, (g + 1) * z.M)
        whole = src_in[rows, :] + landed[:, lane(z, g)]
        value = whole + lifted[:, lane(z, g)]
        if last:
            pairs = lambda p: half_out[p * z.M:(p + 1) * z.M, :]
            src_out[rows, :] = jnp.where(fast, expand(z, rank, pairs, g), value)
            pairs = lambda p: moved[p * z.M:(p + 1) * z.M, :]
            base[rows, :] = start[rows, :] + jnp.where(fast, expand(z, rank, pairs, g), 0.0)
            sources = [x[rows, :] for x in older] + [whole]
            sources = [jnp.where(fast, 0.0, x) for x in sources]
            for k in range(TERMS):
                total = None
                for step, x in zip(range(FINE_STEPS - 1, 0, -1), sources):
                    c = coefficients(step / FINE_STEPS, (step + 1) / FINE_STEPS)[k]
                    total = c * x if total is None else total + c * x
                weights[k, rows, :] = total
        else:
            src_full[rows, :] = whole
            src_out[rows, :] = value


def arrive(z, arrived, landed, stacked):
    for i, group in enumerate(groups_of(z.K, z.Q)):
        for q in range(z.Q):
            rows = min(z.R, (q + 1) * z.QR) - q * z.QR
            landed[q * z.QR:q * z.QR + rows, lane(z, i)] = ungroup(z, [arrived[m] for m in group], q)[0:rows, :]
    hi, lo = halves(landed[...])
    stacked[0:z.R, :] = hi
    stacked[z.RP:z.RP + z.R, :] = lo


def lift_pairs(z, gathered, u, pt):
    low = low_lanes(z, z.BP)
    for c in range(z.C):
        for p in range(z.FP):
            parts = []
            for at in (0, z.RP):
                a = gathered[at + 2 * p * z.BP:at + (2 * p + 1) * z.BP, lane(z, c)]
                b = gathered[at + (2 * p + 1) * z.BP:at + (2 * p + 2) * z.BP, lane(z, c)] if 2 * p + 1 < z.F else 0.0
                parts.append(filled(jnp.where(low, a, b), z.BQ).astype(BF))
            put_face(z, u, c, lane(z, p), *parts)
    return lift(z, pt, u)


def step_kernel(z, first, *refs):
    arrived, refs = refs[:z.K], refs[z.K:]
    half_in, moved_in, s3, p3, pt, star, across, ohr, ohs = refs[:9]
    half, moved, y3, traces, sx, stacked = refs[9:15]
    messages, refs = refs[15:15 + z.K], refs[15 + z.K:]
    landed, gathered, u, turned, other, change, sent, picked = refs
    arrive(z, arrived, landed, stacked)
    gathered[...] = dot(stacked[...], ohr[...])
    gained = lift_pairs(z, gathered, u, pt)
    row = coefficients(0.0, 1.0 / FINE_STEPS)
    for p in range(z.FP):
        rows = slice(p * z.M, (p + 1) * z.M)
        value = half_in[rows, :] + gained[:, lane(z, p)]
        half[rows, :] = value
        put_field(z, y3, p, row[TERMS - 1] * value)

    buffers = (turned, other)

    def product(out, pairs):
        lanes = slice(pairs[0] * z.E, (pairs[-1] + 1) * z.E)
        out[:, lanes] = dot(s3[...], y3[:, lanes])

    tiles = groups_of(z.FP, 2)
    for pairs in tiles:
        product(turned, pairs)
    for k in range(TERMS - 2, -1, -1):
        now, later = buffers if k % 2 == 0 else buffers[::-1]
        for pairs in tiles:
            for p in pairs:
                rows = slice(p * z.M, (p + 1) * z.M)
                total = row[k] * half[rows, :] + star_pair(z, p, now, star)
                if k > 0:
                    put_field(z, y3, p, total)
                else:
                    change[rows, :] = total
            if k > 0:
                product(later, pairs)
    moved[...] = change[...] if first else moved_in[...] + change[...]
    for p in range(z.FP):
        put_field(z, y3, p, change[p * z.M:(p + 1) * z.M, :])
    traces[...] = dot(p3[...], y3[...])
    for pair in groups_of(z.C, 2):
        t = [face_rows(z, traces, c, z.FP) for c in pair]
        for g in range(z.F):
            total = fold(z, *[face_sum(z, across, g, c, t[i]) for i, c in enumerate(pair)])
            sent[g * z.BP:(g + 1) * z.BP, lane(z, pair[0] // 2)] = total
    pack_messages(z, sent, ohs, sx, messages, picked)


def last_kernel(z, *refs):
    arrived, refs = refs[:z.K], refs[z.K:]
    src_in, weights, base, s3, pt, star, ohr, out = refs[:8]
    landed, stacked, gathered, u, lifted, turned, y3, src = refs[8:]
    arrive(z, arrived, landed, stacked)
    gathered[...] = dot(stacked[...], ohr[...])
    lifted[...] = lift_gathered(z, gathered, u, pt)
    row = coefficients(0.0, 1.0 / FINE_STEPS)
    for g in range(z.F):
        rows = slice(g * z.M, (g + 1) * z.M)
        value = src_in[rows, :] + lifted[:, lane(z, g)]
        src[rows, :] = value
        put_field(z, y3, g, weights[TERMS - 1, rows, :] + row[TERMS - 1] * value)

    def term(i, carry):
        c = F32(row[TERMS - 2])
        for k in range(TERMS - 2):
            c = jnp.where(i == TERMS - 2 - k, F32(row[k]), c)
        turned[0:3 * z.M, :] = dot(s3[...], y3[...])
        for group in groups_of(z.F, 2):
            start = [weights[TERMS - 2 - i, g * z.M:(g + 1) * z.M, :] + c * src[g * z.M:(g + 1) * z.M, :] for g in group]
            sums = star_sum(z, start, group, turned, star, z.F)
            mark(turned, 3 * z.M + 8 * i, sums)
            for g, total in zip(group, sums):
                put_field(z, y3, g, total)
                out[g * z.M:(g + 1) * z.M, :] = total
        return carry

    lax.fori_loop(0, TERMS - 1, term, 0)
    out[...] = out[...] + base[...]


def call(kernel, outs, scratch, *args, remote=False):
    place = pl.BlockSpec(memory_space=pltpu.HBM if remote else pltpu.VMEM)
    if remote:
        args = [pltpu.with_memory_space_constraint(x, pltpu.HBM) for x in args]
    vmem = pl.BlockSpec(memory_space=pltpu.VMEM)
    return pl.pallas_call(
        kernel,
        out_shape=[jax.ShapeDtypeStruct(*o) for o in outs],
        in_specs=[place] * len(args),
        out_specs=[vmem] * len(outs),
        scratch_shapes=[pltpu.VMEM(*o) if isinstance(o, tuple) else o for o in scratch],
        compiler_params=pltpu.CompilerParams(vmem_limit_bytes=24 << 20),
        cost_estimate=pl.CostEstimate(flops=1 << 30, bytes_accessed=2 << 20, transcendentals=0),
    )(*args)


def body(
    final_adjoint,
    star_mats,
    deriv_stiff,
    volume_stiffness,
    face_projection,
    flux_local,
    flux_across,
    cluster,
    partner,
    send_slots,
):
    fields, modes, members = final_adjoint.shape
    faces, bases, _ = face_projection.shape
    plan = matchings()
    width = send_slots.shape[1]
    z = Sizes(fields, modes, faces, bases, members, width, len(plan))

    full, half = ((fields * modes, members), F32), ((z.FP * modes, members), F32)
    y3, y3_half = ((3 * z.MP, fields * members), BF), ((3 * z.MP, z.FP * members), BF)
    traces, traces_half = ((faces * z.BP, fields * members), F32), ((faces * z.BP, z.FP * members), F32)
    turned, turned_half = ((3 * modes, fields * members), F32), ((3 * modes, z.FP * members), F32)
    marked = lambda o: ((o[0][0] + 8 * (TERMS - 1), o[0][1]), o[1])
    u, u_half = ((3 * faces * z.BQ, fields * members), BF), ((3 * faces * z.BQ, z.FP * members), BF)
    gathered, lifted = ((2 * z.RP, z.S), F32), ((modes, fields * members), F32)
    landed, stacked = ((z.R, z.KW), F32), ((2 * z.RP, z.KW), BF)
    sx, sx_half = ((2 * z.RP, z.S), BF), ((2 * z.RP, z.S // 2), BF)
    sent, sent_half, picked = ((z.R, z.S), F32), ((z.R, z.S // 2), F32), ((z.R, z.KW), F32)
    messages_out = [((z.QR, members), F32)] * z.K
    wide = ((3 * modes, up(3 * max(z.MP, faces * z.BQ), 128)), F32)
    pairs = lambda n: ((fields, z.FP, n, members), F32)

    def trade(messages):
        return [lax.ppermute(m, axis, links) for m, (axis, links, _) in zip(messages, plan)]

    star = jnp.transpose(star_mats, (1, 2, 0, 3))
    local = jnp.transpose(flux_local, (1, 2, 0, 3))
    across = jnp.transpose(flux_across, (1, 2, 0, 3))
    args = [
        final_adjoint.reshape(fields * modes, members), jnp.transpose(face_projection, (1, 0, 2)), send_slots, across,
        star, local, deriv_stiff, volume_stiffness, partner, cluster.reshape(1, members),
    ]
    like = lambda x: (x.shape, x.dtype)
    (start, star, local, across, deriv, volume, partner, cluster, p3, square, ohs, y3v, tr, sxv, *messages) = call(
        functools.partial(first_kernel, z, plan),
        [like(args[i]) for i in (0, 4, 5, 3, 6, 7, 8, 9)]
        + [((faces * z.BP, 3 * z.MP), BF), ((128, 128), F32), ((z.S, z.KW), BF), y3, traces, sx] + messages_out,
        [like(args[1]), like(args[2]), sent, picked, ((8, z.KW), jnp.int32), wide, pltpu.SemaphoreType.DMA((len(args),))],
        *args, remote=True,
    )
    arrived = trade(messages)
    s3, v3, pt, ohr, ohl, ohr_pairs, ohs_half, ohl_half, index, star_pairs, across_pairs, local_pairs, src, half_src = call(
        functools.partial(first_local_kernel, z, plan),
        [((3 * modes, 3 * z.MP), BF), ((3 * modes, 3 * z.MP), BF), ((modes, 3 * faces * z.BQ), BF), ((z.KW, z.S), BF),
         ((z.S, z.S), BF), ((z.KW, z.S), BF), ((z.S // 2, z.KW), BF), ((z.S // 2, z.S), BF), ((8, members), jnp.int32),
         pairs(3), pairs(faces), pairs(faces), full, half],
        [turned, u, gathered, wide, ((128, 128), F32), ((8, members), F32)],
        deriv, volume, square, partner, cluster, ohs, star, across, local, y3v, tr, sxv,
    )
    moved = jnp.zeros((8, members), F32)
    sources = []
    for step in range(FINE_STEPS - 1, 0, -1):
        half_src, moved, y3v, tr, sxv, stack, *messages = call(
            functools.partial(step_kernel, z, step == FINE_STEPS - 1),
            [half, half, y3_half, traces_half, sx_half, stacked] + messages_out,
            [landed, gathered, u_half, turned_half, turned_half, half, sent_half, picked],
            *arrived, half_src, moved, s3, p3, pt, star_pairs, across_pairs, ohr_pairs, ohs_half,
        )
        arrived = trade(messages)
        last = step == 1
        local_args = [y3v, tr, sxv, v3, pt, star_pairs, local_pairs, ohl_half, index, src, half_src, stack, ohr]
        local_scratch = [turned_half, u, gathered, u_half, lifted, u, gathered, lifted]
        if last:
            src, weights, base, _ = call(
                functools.partial(local_kernel, z, True), [full, ((TERMS,) + full[0], F32), full, half], local_scratch,
                *local_args, *sources, start, moved,
            )
        else:
            whole, src, half_src = call(functools.partial(local_kernel, z, False), [full, full, half], local_scratch, *local_args)
            sources.append(whole)
    (out,) = call(
        functools.partial(last_kernel, z), [full],
        [landed, stacked, gathered, u, lifted, marked(turned), y3, full],
        *arrived, src, weights, base, s3, pt, star, ohr,
    )
    return out.reshape(fields, modes, members)


def solution(mesh):
    in_specs = (
        P(None, None, ("gx", "gy", "gz")),
        P(None, None, None, ("gx", "gy", "gz")),
        P(),
        P(),
        P(),
        P(None, None, None, ("gx", "gy", "gz")),
        P(None, None, None, ("gx", "gy", "gz")),
        P(("gx", "gy", "gz")),
        P(None, ("gx", "gy", "gz")),
        P(None, ("gx", "gy", "gz")),
    )
    out_specs = P(None, None, ("gx", "gy", "gz"))
    return jax.shard_map(body, mesh=mesh, in_specs=in_specs, out_specs=out_specs, check_vma=False)
```

```python
import functools
import math

import jax
import jax.numpy as jnp
from jax import lax
from jax.experimental import pallas as pl
from jax.experimental.pallas import tpu as pltpu
from jax.sharding import PartitionSpec as P

TERMS = 6
FINE_STEPS = 4
BF = jnp.bfloat16
F32 = jnp.float32


def up(n, unit):
    return -(-n // unit) * unit


AXES = ("gx", "gy", "gz")
ORDER = (("gx", 1), ("gz", 1), ("gx", 0), ("gy", 1), ("gy", 0), ("gz", 0))


def matchings():
    plan = []
    for axis in AXES:
        size = lax.axis_size(axis)
        for first in (0, 1):
            links = [(i, i + 1) for i in range(first, size - 1, 2)]
            if not links:
                continue
            if first == 1 and size % 2 == 0:
                links.append((size - 1, 0))
            plan.append((axis, [q for i, j in links for q in ((i, j), (j, i))], first))
    plan.sort(key=lambda entry: ORDER.index((entry[0], entry[2])))
    return plan


def bearings(plan):
    upward, block = [], [jnp.int32(-1)] * 6
    for number, (axis, _, first) in enumerate(plan):
        a, place, size = AXES.index(axis), lax.axis_index(axis), lax.axis_size(axis)
        rises = lax.rem(place, 2) == first
        upward.append((a, rises))
        for side in (0, 1):
            inside = (place > 0) if side == 0 else (place < size - 1)
            used = jnp.logical_and(rises if side == 1 else jnp.logical_not(rises), inside)
            block[2 * a + side] = jnp.where(used, number, block[2 * a + side])
    return upward, block


def coefficients(lower, upper):
    return [(upper ** (k + 1) - lower ** (k + 1)) / math.factorial(k + 1) for k in range(TERMS)]


def halves(x):
    hi = x.astype(BF)
    return hi, (x - hi.astype(F32)).astype(BF)


def dot(a, b):
    return jnp.dot(a, b, preferred_element_type=F32)


class Sizes:
    def __init__(self, fields, modes, faces, bases, members, width, messages):
        self.F, self.M, self.C, self.B, self.E = fields, modes, faces, bases, members
        self.W, self.K = width, messages
        self.H = members // 2
        self.FP = up(fields, 2) // 2
        self.MP = up(modes, 64)
        self.BP = up(bases, 8)
        self.BQ = up(bases, 16)
        self.R = fields * self.BP
        self.RP = up(self.R, 16)
        self.Q = members // width
        self.QR = up(up(self.R, 8 * self.Q) // self.Q, 8)
        self.KW = up(messages * width, 128)
        self.S = faces * members


def filled(x, rows):
    if x.shape[0] == rows:
        return x
    return jnp.concatenate([x, jnp.zeros((rows - x.shape[0], x.shape[1]), x.dtype)], axis=0)


def put_field(z, y3, f, x):
    hi, lo = halves(filled(x, z.MP))
    lanes = slice(f * z.E, (f + 1) * z.E)
    y3[0:z.MP, lanes] = hi
    y3[z.MP:2 * z.MP, lanes] = lo
    y3[2 * z.MP:3 * z.MP, lanes] = hi


def put_face(z, u, c, lanes, hi, lo):
    for part, value in enumerate((hi, lo, hi)):
        at = (part * z.C + c) * z.BQ
        u[at:at + z.BQ, lanes] = value


def lift(z, pt, u):
    return dot(pt[...], u[...])


def lane(z, i):
    return slice(i * z.E, (i + 1) * z.E)


def take(x, row):
    return jnp.take_along_axis(x, jnp.broadcast_to(row, x.shape), axis=1)


def low_lanes(z, rows):
    return lax.broadcasted_iota(jnp.int32, (rows, z.E), 1) < z.H


def balanced(z, out, matrix, y3):
    rows, lanes = matrix.shape[0], out.shape[1]
    even = lanes // (2 * z.E) * 2 * z.E
    out[0:rows, 0:even] = dot(matrix[...], y3[:, 0:even])
    if even < lanes:
        cut = up(rows // 2, 16)
        out[0:cut, even:lanes] = dot(matrix[0:cut, :], y3[:, even:lanes])
        out[cut:rows, even:lanes] = dot(matrix[cut:rows, :], y3[:, even:lanes])


def fold(z, first, second):
    low = low_lanes(z, first.shape[0])
    second = jnp.zeros_like(first) if second is None else second
    return jnp.where(low, first, second) + pltpu.roll(jnp.where(low, second, first), z.H, 1)


def compact(z, pick, field):
    low = low_lanes(z, z.M)
    out = []
    for p in range(z.FP):
        a = take(field(2 * p), pick)
        b = take(field(2 * p + 1), pick) if 2 * p + 1 < z.F else jnp.zeros_like(a)
        out.append(jnp.where(low, a, b))
    return out


def expand(z, rank, pairs, f):
    return take(pairs(f // 2), rank + z.H * (f % 2))


def star_sum(z, start, group, turned, star, count):
    total = list(start)
    for f in range(count):
        for d in range(3):
            t = turned[d * z.M:(d + 1) * z.M, lane(z, f)]
            for i, g in enumerate(group):
                term = star[g, f, d:d + 1, :] * t
                total[i] = term if total[i] is None else total[i] + term
    return total


def mark(ref, at, parts):
    for i, x in enumerate(parts):
        ref[pl.ds(pl.multiple_of(at, 8), 8), i * x.shape[1]:(i + 1) * x.shape[1]] = x[0:8, :]


def star_pair(z, p, turned, star):
    group = [g for g in (2 * p, 2 * p + 1) if g < z.F]
    total = star_sum(z, [None] * len(group), group, turned, star, z.FP)
    return fold(z, total[0], total[1] if len(group) == 2 else None)


def face_sum(z, flux, g, c, t):
    total = flux[g, 0, c:c + 1, :] * t[0]
    for f in range(1, len(t)):
        total = total + flux[g, f, c:c + 1, :] * t[f]
    return total


def face_rows(z, traces, c, count):
    return [traces[c * z.BP:(c + 1) * z.BP, lane(z, f)] for f in range(count)]


def groups_of(n, size):
    return [list(range(i, min(n, i + size))) for i in range(0, n, size)]


def regroup(z, base, part):
    group = lax.broadcasted_iota(jnp.int32, (z.QR, z.E), 1)
    out = None
    for q in range(z.Q):
        shift = (q - base) % z.Q * z.W
        x = part(q)
        x = pltpu.roll(x, shift, 1) if shift else x
        out = x if out is None else jnp.where(group >= q * z.W, x, out)
    return out


def ungroup(z, messages, q):
    group = lax.broadcasted_iota(jnp.int32, (z.QR, z.E), 1)
    out = None
    for m, message in enumerate(messages):
        shift = (m - q) % z.Q * z.W
        x = message[...]
        x = pltpu.roll(x, shift, 1) if shift else x
        out = x if out is None else jnp.where(group >= m * z.W, x, out)
    if len(messages) < z.Q:
        out = jnp.where(group < len(messages) * z.W, out, 0.0)
    return out


def pack_messages(z, sent, ohs, sx, messages, picked):
    hi, lo = halves(sent[...])
    sx[0:z.R, :] = hi
    sx[z.RP:z.RP + z.R, :] = lo
    both = dot(sx[...], ohs[...])
    picked[...] = both[0:z.R, :] + both[z.RP:z.RP + z.R, :]
    for m, message in enumerate(messages):
        home = lane(z, m // z.Q)
        message[...] = regroup(z, m % z.Q, lambda q: filled(picked[q * z.QR:min(z.R, (q + 1) * z.QR), home], z.QR))


def triple(rows, cols, target, wide, matrix):
    hi = matrix.astype(BF).astype(F32)
    wide[rows, 0:cols] = hi
    wide[rows, cols:2 * cols] = hi
    wide[rows, 2 * cols:3 * cols] = matrix - hi
    target[rows, :] = wide[rows, 0:3 * cols].astype(BF)


def first_kernel(z, plan, *refs):
    n = 10
    hbm, refs = refs[:n], refs[n:]
    (y, star, local, across, deriv, volume, partner, cluster, p3, square, ohs, y3, traces, sx), refs = refs[:14], refs[14:]
    messages, refs = refs[:z.K], refs[z.K:]
    projection, slots, sent, picked, picks, wide, sem = refs
    targets = (y, projection, slots, across, star, local, deriv, volume, partner, cluster)
    copies = [pltpu.make_async_copy(a, b, sem.at[i]) for i, (a, b) in enumerate(zip(hbm, targets))]
    for i in (2, 1, 0, 3, *range(4, n)):
        copies[i].start()
    square[...] = jnp.zeros_like(square)
    wide[...] = jnp.zeros_like(wide)
    picks[...] = jnp.full_like(picks, -1)
    copies[1].wait()
    for c in range(z.C):
        for b in range(z.B):
            square[c * z.BQ + b:c * z.BQ + b + 1, 0:z.M] = projection[b, c:c + 1, :]
    for c in range(z.C):
        rows = slice(c * z.BP, (c + 1) * z.BP)
        triple(rows, z.MP, p3, wide, square[c * z.BQ:c * z.BQ + z.BP, 0:z.MP])
    copies[0].wait()
    for f in range(z.F):
        put_field(z, y3, f, y[f * z.M:(f + 1) * z.M, :])
    copies[3].wait()
    upward, _ = bearings(plan)
    copies[2].wait()
    for m, (a, rises) in enumerate(upward):
        picks[0:1, m * z.W:(m + 1) * z.W] = jnp.where(rises, slots[2 * a + 1:2 * a + 2, :], slots[2 * a:2 * a + 1, :])
    ids = lax.broadcasted_iota(jnp.int32, (z.S, z.KW), 0)
    ohs[...] = jnp.where(ids == picks[0:1, :], 1.0, 0.0).astype(BF)
    traces[...] = dot(p3[...], y3[...])
    for c in range(z.C):
        t = face_rows(z, traces, c, z.F)
        for g in range(z.F):
            sent[g * z.BP:(g + 1) * z.BP, lane(z, c)] = face_sum(z, across, g, c, t)
    pack_messages(z, sent, ohs, sx, messages, picked)
    for copy in copies[4:]:
        copy.wait()


def set_up(z, plan, deriv, volume, square, partner, cluster, ohs, star, across, local, outs, scratch):
    s3, v3, pt, ohr, ohl, ohr_pairs, ohs_half, ohl_half, index, star_pairs, across_pairs, local_pairs = outs
    wide, block, picks = scratch
    wide[...] = jnp.zeros_like(wide)
    block[...] = jnp.zeros_like(block)
    for source, target in ((deriv, s3), (volume, v3)):
        for d in range(3):
            block[0:z.M, 0:z.M] = source[d]
            turned = jnp.transpose(block[...])
            triple(slice(d * z.M, (d + 1) * z.M), z.MP, target, wide, turned[0:z.M, 0:z.MP])
    triple(slice(0, z.M), z.C * z.BQ, pt, wide, jnp.transpose(square[...])[0:z.M, 0:z.C * z.BQ])
    _, arrival = bearings(plan)
    far = partner[...] - z.S
    moved = jnp.full_like(far, -1)
    for i in range(6):
        here = jnp.logical_and(far >= i * z.W, far < (i + 1) * z.W)
        here = jnp.logical_and(here, arrival[i] >= 0)
        moved = jnp.where(here, arrival[i] * z.W + far - i * z.W, moved)
    slots = partner[...]
    for c in range(z.C):
        ids = lax.broadcasted_iota(jnp.int32, (z.S, z.E), 0)
        ohl[:, lane(z, c)] = jnp.where(ids == slots[c:c + 1, :], 1.0, 0.0).astype(BF)
        ids = lax.broadcasted_iota(jnp.int32, (z.KW, z.E), 0)
        ohr[:, lane(z, c)] = jnp.where(ids == moved[c:c + 1, :], 1.0, 0.0).astype(BF)
    fast = cluster[...] == 0
    flags = jnp.broadcast_to(jnp.where(fast, 1.0, 0.0), (8, z.E))
    a = lax.broadcasted_iota(jnp.int32, (z.E, z.E), 0)
    b = lax.broadcasted_iota(jnp.int32, (z.E, z.E), 1)
    below = jnp.where(a <= b, 1.0, 0.0).astype(BF)
    running = dot(flags.astype(BF), below)
    count = dot(flags.astype(BF), jnp.ones((z.E, z.E), BF))
    rank = running[0:1, :].astype(jnp.int32) - 1
    held = jnp.where(fast, rank, -1)
    chosen = jnp.where(lax.broadcasted_iota(jnp.int32, (z.H, z.E), 0) == held, 1.0, 0.0).astype(BF)
    numbers = lax.broadcasted_iota(jnp.int32, (8, z.E), 1).astype(F32).astype(BF)
    listed = lax.dot_general(numbers, chosen, (((1,), (1,)), ((), ())), preferred_element_type=F32)
    picks[:, 0:z.H] = listed
    picks[:, z.H:2 * z.H] = listed
    pick = picks[0:1, :].astype(jnp.int32)
    place = lax.broadcasted_iota(jnp.int32, (1, z.E), 1)
    place = jnp.where(place < z.H, place, place - z.H)
    live = place < count[0:1, :].astype(jnp.int32)
    index[...] = jnp.zeros_like(index)
    index[0:1, :] = pick
    index[1:2, :] = jnp.maximum(rank, 0)
    index[2:3, :] = jnp.where(fast, 1, 0)
    both = jnp.concatenate([chosen, chosen], axis=0)
    for c in range(z.C):
        pairs = lax.dot_general(ohr[:, lane(z, c)], both, (((1,), (1,)), ((), ())), preferred_element_type=F32)
        ohr_pairs[:, lane(z, c)] = pairs.astype(BF)
        rows = slice(c * z.H, (c + 1) * z.H)
        ohs_half[rows, :] = dot(chosen, ohs[lane(z, c), :]).astype(BF)
        ohl_half[rows, :] = dot(chosen, ohl[lane(z, c), :]).astype(BF)
    for source, target in ((star, star_pairs), (across, across_pairs), (local, local_pairs)):
        low = jnp.logical_and(low_lanes(z, 1), live)
        high = jnp.logical_and(jnp.logical_not(low_lanes(z, 1)), live)
        for g in range(z.F):
            for p in range(z.FP):
                value = jnp.where(low, take(source[g, 2 * p], pick), 0.0)
                if 2 * p + 1 < z.F:
                    value = jnp.where(high, take(source[g, 2 * p + 1], pick), value)
                target[g, p] = value


def first_local_kernel(z, plan, *refs):
    deriv, volume, square, partner, cluster, ohs, star, across, local, y3, traces, sx = refs[:12]
    outs, src, half, refs = refs[12:24], refs[24], refs[25], refs[26:]
    turned, u, gathered, *scratch = refs
    set_up(z, plan, deriv, volume, square, partner, cluster, ohs, star, across, local, outs, scratch)
    v3, pt, ohl = outs[1], outs[2], outs[4]
    turned[...] = dot(v3[...], y3[...])
    gathered[...] = dot(sx[...], ohl[...])
    for c in range(z.C):
        t = face_rows(z, traces, c, z.F)
        for g in range(z.F):
            total = gathered[g * z.BP:(g + 1) * z.BP, lane(z, c)] + gathered[z.RP + g * z.BP:z.RP + (g + 1) * z.BP, lane(z, c)]
            hi, lo = halves(filled(total + face_sum(z, local, g, c, t), z.BQ))
            put_face(z, u, c, lane(z, g), hi, lo)
    lifted = lift(z, pt, u)
    for group in groups_of(z.F, 3):
        start = [lifted[:, lane(z, g)] for g in group]
        for g, total in zip(group, star_sum(z, start, group, turned, star, z.F)):
            src[g * z.M:(g + 1) * z.M, :] = total
    index = outs[8]
    for p, value in enumerate(compact(z, index[0:1, :], lambda f: src[f * z.M:(f + 1) * z.M, :])):
        half[p * z.M:(p + 1) * z.M, :] = value


def lift_gathered(z, gathered, u, pt):
    for c in range(z.C):
        for g in range(z.F):
            hi = filled(gathered[g * z.BP:(g + 1) * z.BP, lane(z, c)], z.BQ).astype(BF)
            lo = filled(gathered[z.RP + g * z.BP:z.RP + (g + 1) * z.BP, lane(z, c)], z.BQ).astype(BF)
            put_face(z, u, c, lane(z, g), hi, lo)
    return lift(z, pt, u)


def local_kernel(z, step, *refs):
    y3, traces, sx, v3, pt, star, local, ohl, index, src_in, half_in, stacked, ohr = refs[:13]
    refs = refs[13:]
    last = step == 1
    if last:
        partial, start, moved, src_out, weights, base, half_out = refs[:7]
        refs = refs[7:]
    elif step == 2:
        older, partial, src_out, half_out = refs[:4]
        refs = refs[4:]
    else:
        src_full, src_out, half_out = refs[:3]
        refs = refs[3:]
    shares = [coefficients(i / FINE_STEPS, (i + 1) / FINE_STEPS) for i in range(FINE_STEPS)]
    turned, u, gathered, u_half, lifted, u_far, gathered_far, landed = refs
    gathered_far[...] = dot(stacked[...], ohr[...])
    landed[...] = lift_gathered(z, gathered_far, u_far, pt)
    turned[...] = dot(v3[...], y3[...])
    gathered[...] = dot(sx[...], ohl[...])
    for c in range(z.C):
        t = face_rows(z, traces, c, z.FP)
        for p in range(z.FP):
            first = face_sum(z, local, 2 * p, c, t)
            second = face_sum(z, local, 2 * p + 1, c, t) if 2 * p + 1 < z.F else None
            hi, lo = halves(filled(fold(z, first, second), z.BQ))
            put_face(z, u_half, c, lane(z, p), hi, lo)
    lifted_half = lift(z, pt, u_half)
    lifted[...] = lift_gathered(z, gathered, u, pt)
    pick, rank = index[0:1, :], index[1:2, :]
    gained = compact(z, pick, lambda f: lifted[:, lane(z, f)])
    for p in range(z.FP):
        rows = slice(p * z.M, (p + 1) * z.M)
        half_out[rows, :] = half_in[rows, :] + gained[p] + lifted_half[:, lane(z, p)] + star_pair(z, p, turned, star)
    fast = index[2:3, :] > 0
    for g in range(z.F):
        rows = slice(g * z.M, (g + 1) * z.M)
        whole = src_in[rows, :] + landed[:, lane(z, g)]
        value = whole + lifted[:, lane(z, g)]
        if last:
            pairs = lambda p: half_out[p * z.M:(p + 1) * z.M, :]
            src_out[rows, :] = jnp.where(fast, expand(z, rank, pairs, g), value)
            pairs = lambda p: moved[p * z.M:(p + 1) * z.M, :]
            base[rows, :] = start[rows, :] + jnp.where(fast, expand(z, rank, pairs, g), 0.0)
            slow = jnp.where(fast, 0.0, whole)
            for k in range(TERMS):
                weights[k, rows, :] = partial[k, rows, :] + shares[1][k] * slow
        elif step == 2:
            src_out[rows, :] = value
            before = jnp.where(fast, 0.0, older[rows, :])
            slow = jnp.where(fast, 0.0, whole)
            for k in range(TERMS):
                partial[k, rows, :] = shares[3][k] * before + shares[2][k] * slow
        else:
            src_full[rows, :] = whole
            src_out[rows, :] = value


def arrive(z, arrived, landed, stacked):
    for i, group in enumerate(groups_of(z.K, z.Q)):
        for q in range(z.Q):
            rows = min(z.R, (q + 1) * z.QR) - q * z.QR
            landed[q * z.QR:q * z.QR + rows, lane(z, i)] = ungroup(z, [arrived[m] for m in group], q)[0:rows, :]
    hi, lo = halves(landed[...])
    stacked[0:z.R, :] = hi
    stacked[z.RP:z.RP + z.R, :] = lo


def lift_pairs(z, gathered, u, pt):
    low = low_lanes(z, z.BP)
    for c in range(z.C):
        for p in range(z.FP):
            parts = []
            for at in (0, z.RP):
                a = gathered[at + 2 * p * z.BP:at + (2 * p + 1) * z.BP, lane(z, c)]
                b = gathered[at + (2 * p + 1) * z.BP:at + (2 * p + 2) * z.BP, lane(z, c)] if 2 * p + 1 < z.F else 0.0
                parts.append(filled(jnp.where(low, a, b), z.BQ).astype(BF))
            put_face(z, u, c, lane(z, p), *parts)
    return lift(z, pt, u)


def step_kernel(z, first, *refs):
    arrived, refs = refs[:z.K], refs[z.K:]
    half_in, moved_in, s3, p3, pt, star, across, ohr, ohs = refs[:9]
    half, moved, y3, traces, sx, stacked = refs[9:15]
    messages, refs = refs[15:15 + z.K], refs[15 + z.K:]
    landed, gathered, u, turned, other, change, sent, picked = refs
    arrive(z, arrived, landed, stacked)
    gathered[...] = dot(stacked[...], ohr[...])
    gained = lift_pairs(z, gathered, u, pt)
    row = coefficients(0.0, 1.0 / FINE_STEPS)
    for p in range(z.FP):
        rows = slice(p * z.M, (p + 1) * z.M)
        value = half_in[rows, :] + gained[:, lane(z, p)]
        half[rows, :] = value
        put_field(z, y3, p, row[TERMS - 1] * value)

    buffers = (turned, other)

    def product(out, pairs):
        lanes = slice(pairs[0] * z.E, (pairs[-1] + 1) * z.E)
        out[:, lanes] = dot(s3[...], y3[:, lanes])

    tiles = groups_of(z.FP, 2)
    for pairs in tiles:
        product(turned, pairs)
    for k in range(TERMS - 2, -1, -1):
        now, later = buffers if k % 2 == 0 else buffers[::-1]
        for pairs in tiles:
            for p in pairs:
                rows = slice(p * z.M, (p + 1) * z.M)
                total = row[k] * half[rows, :] + star_pair(z, p, now, star)
                if k > 0:
                    put_field(z, y3, p, total)
                else:
                    change[rows, :] = total
            if k > 0:
                product(later, pairs)
    moved[...] = change[...] if first else moved_in[...] + change[...]
    for p in range(z.FP):
        put_field(z, y3, p, change[p * z.M:(p + 1) * z.M, :])
    traces[...] = dot(p3[...], y3[...])
    for pair in groups_of(z.C, 2):
        t = [face_rows(z, traces, c, z.FP) for c in pair]
        for g in range(z.F):
            total = fold(z, *[face_sum(z, across, g, c, t[i]) for i, c in enumerate(pair)])
            sent[g * z.BP:(g + 1) * z.BP, lane(z, pair[0] // 2)] = total
    pack_messages(z, sent, ohs, sx, messages, picked)


def last_kernel(z, *refs):
    arrived, refs = refs[:z.K], refs[z.K:]
    src_in, weights, base, s3, pt, star, ohr, out = refs[:8]
    landed, stacked, gathered, u, lifted, turned, y3, src = refs[8:]
    arrive(z, arrived, landed, stacked)
    gathered[...] = dot(stacked[...], ohr[...])
    lifted[...] = lift_gathered(z, gathered, u, pt)
    row = coefficients(0.0, 1.0 / FINE_STEPS)
    for g in range(z.F):
        rows = slice(g * z.M, (g + 1) * z.M)
        value = src_in[rows, :] + lifted[:, lane(z, g)]
        src[rows, :] = value
        put_field(z, y3, g, weights[TERMS - 1, rows, :] + row[TERMS - 1] * value)

    def term(i, carry):
        c = F32(row[TERMS - 2])
        for k in range(TERMS - 2):
            c = jnp.where(i == TERMS - 2 - k, F32(row[k]), c)
        turned[0:3 * z.M, :] = dot(s3[...], y3[...])
        for group in groups_of(z.F, 2):
            start = [weights[TERMS - 2 - i, g * z.M:(g + 1) * z.M, :] + c * src[g * z.M:(g + 1) * z.M, :] for g in group]
            sums = star_sum(z, start, group, turned, star, z.F)
            mark(turned, 3 * z.M + 8 * i, sums)
            for g, total in zip(group, sums):
                put_field(z, y3, g, total)
                out[g * z.M:(g + 1) * z.M, :] = total
        return carry

    lax.fori_loop(0, TERMS - 1, term, 0)
    out[...] = out[...] + base[...]


def call(kernel, outs, scratch, *args, remote=False):
    place = pl.BlockSpec(memory_space=pltpu.HBM if remote else pltpu.VMEM)
    if remote:
        args = [pltpu.with_memory_space_constraint(x, pltpu.HBM) for x in args]
    vmem = pl.BlockSpec(memory_space=pltpu.VMEM)
    return pl.pallas_call(
        kernel,
        out_shape=[jax.ShapeDtypeStruct(*o) for o in outs],
        in_specs=[place] * len(args),
        out_specs=[vmem] * len(outs),
        scratch_shapes=[pltpu.VMEM(*o) if isinstance(o, tuple) else o for o in scratch],
        compiler_params=pltpu.CompilerParams(vmem_limit_bytes=24 << 20),
        cost_estimate=pl.CostEstimate(flops=1 << 30, bytes_accessed=2 << 20, transcendentals=0),
    )(*args)


def body(
    final_adjoint,
    star_mats,
    deriv_stiff,
    volume_stiffness,
    face_projection,
    flux_local,
    flux_across,
    cluster,
    partner,
    send_slots,
):
    fields, modes, members = final_adjoint.shape
    faces, bases, _ = face_projection.shape
    plan = matchings()
    width = send_slots.shape[1]
    z = Sizes(fields, modes, faces, bases, members, width, len(plan))

    full, half = ((fields * modes, members), F32), ((z.FP * modes, members), F32)
    y3, y3_half = ((3 * z.MP, fields * members), BF), ((3 * z.MP, z.FP * members), BF)
    traces, traces_half = ((faces * z.BP, fields * members), F32), ((faces * z.BP, z.FP * members), F32)
    turned, turned_half = ((3 * modes, fields * members), F32), ((3 * modes, z.FP * members), F32)
    marked = lambda o: ((o[0][0] + 8 * (TERMS - 1), o[0][1]), o[1])
    u, u_half = ((3 * faces * z.BQ, fields * members), BF), ((3 * faces * z.BQ, z.FP * members), BF)
    gathered, lifted = ((2 * z.RP, z.S), F32), ((modes, fields * members), F32)
    landed, stacked = ((z.R, z.KW), F32), ((2 * z.RP, z.KW), BF)
    sx, sx_half = ((2 * z.RP, z.S), BF), ((2 * z.RP, z.S // 2), BF)
    sent, sent_half, picked = ((z.R, z.S), F32), ((z.R, z.S // 2), F32), ((z.R, z.KW), F32)
    messages_out = [((z.QR, members), F32)] * z.K
    wide = ((3 * modes, up(3 * max(z.MP, faces * z.BQ), 128)), F32)
    pairs = lambda n: ((fields, z.FP, n, members), F32)

    def trade(messages):
        return [lax.ppermute(m, axis, links) for m, (axis, links, _) in zip(messages, plan)]

    star = jnp.transpose(star_mats, (1, 2, 0, 3))
    local = jnp.transpose(flux_local, (1, 2, 0, 3))
    across = jnp.transpose(flux_across, (1, 2, 0, 3))
    args = [
        final_adjoint.reshape(fields * modes, members), jnp.transpose(face_projection, (1, 0, 2)), send_slots, across,
        star, local, deriv_stiff, volume_stiffness, partner, cluster.reshape(1, members),
    ]
    like = lambda x: (x.shape, x.dtype)
    (start, star, local, across, deriv, volume, partner, cluster, p3, square, ohs, y3v, tr, sxv, *messages) = call(
        functools.partial(first_kernel, z, plan),
        [like(args[i]) for i in (0, 4, 5, 3, 6, 7, 8, 9)]
        + [((faces * z.BP, 3 * z.MP), BF), ((128, 128), F32), ((z.S, z.KW), BF), y3, traces, sx] + messages_out,
        [like(args[1]), like(args[2]), sent, picked, ((8, z.KW), jnp.int32), wide, pltpu.SemaphoreType.DMA((len(args),))],
        *args, remote=True,
    )
    arrived = trade(messages)
    s3, v3, pt, ohr, ohl, ohr_pairs, ohs_half, ohl_half, index, star_pairs, across_pairs, local_pairs, src, half_src = call(
        functools.partial(first_local_kernel, z, plan),
        [((3 * modes, 3 * z.MP), BF), ((3 * modes, 3 * z.MP), BF), ((modes, 3 * faces * z.BQ), BF), ((z.KW, z.S), BF),
         ((z.S, z.S), BF), ((z.KW, z.S), BF), ((z.S // 2, z.KW), BF), ((z.S // 2, z.S), BF), ((8, members), jnp.int32),
         pairs(3), pairs(faces), pairs(faces), full, half],
        [turned, u, gathered, wide, ((128, 128), F32), ((8, members), F32)],
        deriv, volume, square, partner, cluster, ohs, star, across, local, y3v, tr, sxv,
    )
    moved = jnp.zeros((8, members), F32)
    for step in range(FINE_STEPS - 1, 0, -1):
        half_src, moved, y3v, tr, sxv, stack, *messages = call(
            functools.partial(step_kernel, z, step == FINE_STEPS - 1),
            [half, half, y3_half, traces_half, sx_half, stacked] + messages_out,
            [landed, gathered, u_half, turned_half, turned_half, half, sent_half, picked],
            *arrived, half_src, moved, s3, p3, pt, star_pairs, across_pairs, ohr_pairs, ohs_half,
        )
        arrived = trade(messages)
        last = step == 1
        local_args = [y3v, tr, sxv, v3, pt, star_pairs, local_pairs, ohl_half, index, src, half_src, stack, ohr]
        local_scratch = [turned_half, u, gathered, u_half, lifted, u, gathered, lifted]
        if last:
            src, weights, base, _ = call(
                functools.partial(local_kernel, z, step), [full, ((TERMS,) + full[0], F32), full, half], local_scratch,
                *local_args, partial, start, moved,
            )
        elif step == 2:
            partial, src, half_src = call(
                functools.partial(local_kernel, z, step), [((TERMS,) + full[0], F32), full, half], local_scratch,
                *local_args, whole,
            )
        else:
            whole, src, half_src = call(functools.partial(local_kernel, z, step), [full, full, half], local_scratch, *local_args)
    (out,) = call(
        functools.partial(last_kernel, z), [full],
        [landed, stacked, gathered, u, lifted, marked(turned), y3, full],
        *arrived, src, weights, base, s3, pt, star, ohr,
    )
    return out.reshape(fields, modes, members)


def solution(mesh):
    in_specs = (
        P(None, None, ("gx", "gy", "gz")),
        P(None, None, None, ("gx", "gy", "gz")),
        P(),
        P(),
        P(),
        P(None, None, None, ("gx", "gy", "gz")),
        P(None, None, None, ("gx", "gy", "gz")),
        P(("gx", "gy", "gz")),
        P(None, ("gx", "gy", "gz")),
        P(None, ("gx", "gy", "gz")),
    )
    out_specs = P(None, None, ("gx", "gy", "gz"))
    return jax.shard_map(body, mesh=mesh, in_specs=in_specs, out_specs=out_specs, check_vma=False)
```
